256 devices in a mesh: ty: 16 (over y, x_hi, core), tx: 16 (over z, x_lo).
Axes of the slice: x: 4 (x_hi: 2, x_lo: 2; x = x_hi * 2 + x_lo), y: 4, z: 8, core: 2. Of those that a mesh axis runs over, the one named last changes fastest.
Arguments:
- block_input: bfloat16 [1024, 768, 256], P('ty', 'tx'), may hold values from -6 to 6
- cotangent: bfloat16 [1024, 768, 256], P('ty', 'tx'), may hold values from -6 to 6
- tissue: int32 [64, 48], P('ty', 'tx'), may hold values 0 or 1
- dw_weight: float32 [49, 256], replicated, may hold values from -0.875 to 0.875
- dw_bias: float32 [256], replicated, may hold values from -3 to 3
- ln_gain: float32 [256], replicated, may hold values from 0.5 to 1.5
- ln_bias: float32 [256], replicated, may hold values from -3 to 3
- w_expand: bfloat16 [256, 1024], replicated, may hold values from -0.375 to 0.375
- b_expand: float32 [1024], replicated, may hold values from -3 to 3
- w_reduce: bfloat16 [1024, 256], replicated, may hold values from -0.1875 to 0.1875
- layer_scale: float32 [256], replicated, may hold values from 0.5 to 2
Outputs:
- grad_input: bfloat16 [1024, 768, 256], P('ty', 'tx')
- grad_dw: float32 [49, 256], replicated
- grad_expand: float32 [256, 1024], replicated
- grad_reduce: float32 [1024, 256], replicated
The draws below stay inside these ranges and needn't reach their ends.
Inputs may be any that keep to these rules, and one draw needn't show every extreme that they name: 1 marks a tile with tissue.
All inputs are finite; a program needn't handle non-finite values. No bound on the sum of `tissue` on one device may be relied on, other than what follows from the above.
Results may differ from the reference program's by a relative error of at most 0.007.
Values may be sent and summed in bfloat16 or wider, within the bound.
No kernel may reach another device: no remote copies, remote signals or barrier semaphores. Data moves between devices by JAX's collectives and lax.ppermute only.
A program may use at most 256 MiB of HBM per device.

```python
import math
import jax
import jax.numpy as jnp
from jax import lax

C = 256
HID = 1024
TILE = 16
BH = 64
H = 1024
W = 768
N_TY = 16


def place_ends(array, own_key, low, largest):
    spot = [jax.random.randint(jax.random.fold_in(own_key, axis), (), 0, length) for axis, length in enumerate(array.shape)]
    longest = array.shape.index(max(array.shape))
    beside = spot[:longest] + [(spot[longest] + 1) % array.shape[longest]] + spot[longest + 1:]
    return array.at[tuple(spot)].set(low).at[tuple(beside)].set(largest)


def block_levels(own_key, extent, split, low, high):
    factor_of, own = 1.0, jax.random.fold_in(own_key, 6)
    for dim, parts in split:
        heights = jnp.exp(jax.random.uniform(jax.random.fold_in(own, dim), (parts,), jnp.float32, low / len(split), high / len(split)))
        factor_of = factor_of * jnp.repeat(heights, extent[dim] // parts).reshape([-1 if axis == dim else 1 for axis in range(len(extent))])
    return factor_of


def scatter_about(own_key, extent, scale, most, split=(), held_as=jnp.bfloat16):
    values = jax.random.normal(own_key, extent, jnp.float32) * scale
    if len(split) > 0:
        values = block_levels(own_key, extent, split, -0.22, 0.18) * values
    return jnp.clip(values, min=-most, max=most).astype(held_as)


def setup_inputs(seed: int = 0) -> dict:
    streams_of = jax.random.split(jax.random.key(seed), 12)
    return {
        "block_input": scatter_about(streams_of[0], (H, W, C), 1.0, 6.0, ((0, 16), (1, 16))),
        "cotangent": scatter_about(streams_of[1], (H, W, C), 1.0, 6.0, ((0, 16), (1, 16))),
        "tissue": place_ends((jax.random.randint(streams_of[2], (H // TILE, W // TILE), 0, 2) < 1).astype(jnp.int32), jax.random.fold_in(streams_of[2], 1), 0, 1),
        "dw_weight": scatter_about(streams_of[3], (49, C), 49 ** -0.5, 0.875, (), jnp.float32),
        "dw_bias": scatter_about(streams_of[4], (C,), 0.5, 3.0, (), jnp.float32),
        "ln_gain": jnp.clip(jax.random.uniform(streams_of[5], (C,), jnp.float32, 0.5, 1.5), 0.5, 1.5),
        "ln_bias": scatter_about(streams_of[6], (C,), 0.5, 3.0, (), jnp.float32),
        "w_expand": scatter_about(streams_of[7], (C, HID), C ** -0.5, 0.375),
        "b_expand": scatter_about(streams_of[8], (HID,), 0.5, 3.0, (), jnp.float32),
        "w_reduce": scatter_about(streams_of[9], (HID, C), HID ** -0.5, 0.1875),
        "layer_scale": jnp.clip(jnp.exp(jax.random.uniform(streams_of[10], (C,), jnp.float32, math.log(0.5), math.log(2.0))), 0.5, 2.0),
    }


def depthwise(padded, kernel, rows, cols):
    total = jnp.zeros((rows, cols, padded.shape[2]), jnp.float32)
    for row_off in range(7):
        for col_off in range(7):
            window = padded[row_off:row_off + rows, col_off:col_off + cols].astype(jnp.float32)
            total = total + window * kernel[row_off * 7 + col_off]
    return total

def filter_grad(padded, grad, rows, cols):
    gradf = grad.astype(jnp.float32)
    taps = []
    for row_off in range(7):
        for col_off in range(7):
            window = padded[row_off:row_off + rows, col_off:col_off + cols].astype(jnp.float32)
            taps.append(lax.optimization_barrier(jnp.sum(window * gradf, axis=(0, 1))))
    return jnp.stack(taps)

def branch_back(pre, masked, ln_gain, ln_bias, w_expand, b_expand, w_reduce, layer_scale):
    center = pre - lax.optimization_barrier(jnp.mean(pre, axis=-1, keepdims=True))
    rstd = lax.rsqrt(lax.optimization_barrier(jnp.mean(center * center, axis=-1, keepdims=True)) + 1e-06)
    nhat = center * rstd
    normed = (nhat * ln_gain + ln_bias).astype(jnp.bfloat16)
    zvals = jnp.dot(normed, w_expand, preferred_element_type=jnp.float32) + b_expand
    cdf = 0.5 * (1.0 + jax.scipy.special.erf(zvals * 0.7071067811865476))
    hidden = (zvals * cdf).astype(jnp.bfloat16)
    go_vals = (layer_scale * masked.astype(jnp.float32)).astype(jnp.bfloat16)
    dhid = jnp.dot(go_vals, w_reduce.T, preferred_element_type=jnp.float32)
    slope = cdf + zvals * jnp.exp(-0.5 * zvals * zvals) * 0.3989422804014327
    dzvals = (dhid * slope).astype(jnp.bfloat16)
    dnorm = jnp.dot(dzvals, w_expand.T, preferred_element_type=jnp.float32) * ln_gain
    grad = rstd * (dnorm - lax.optimization_barrier(jnp.mean(dnorm, axis=-1, keepdims=True)) - nhat * lax.optimization_barrier(jnp.mean(dnorm * nhat, axis=-1, keepdims=True)))
    return (grad.astype(jnp.bfloat16), hidden, normed, go_vals, dzvals)

def reference(block_input, cotangent, tissue, dw_weight, dw_bias, ln_gain, ln_bias, w_expand, b_expand, w_reduce, layer_scale):
    mask = jnp.repeat(jnp.repeat(tissue, TILE, axis=0), TILE, axis=1)
    masked = (cotangent.astype(jnp.float32) * mask[:, :, None].astype(jnp.float32)).astype(jnp.bfloat16)
    padded = jnp.pad(block_input, ((3, 3), (3, 3), (0, 0)))
    zero = jnp.int32(0)

    def band_step(carry, index):
        acc_expand, acc_reduce, acc_dw = carry
        start = (index * BH).astype(jnp.int32)
        band = lax.dynamic_slice(padded, (start, zero, zero), (BH + 6, W + 6, C))
        pre = depthwise(band, dw_weight, BH, W) + dw_bias
        mband = lax.dynamic_slice(masked, (start, zero, zero), (BH, W, C))
        grad, hidden, normed, go_vals, dzvals = branch_back(pre.reshape(-1, C), mband.reshape(-1, C), ln_gain, ln_bias, w_expand, b_expand, w_reduce, layer_scale)
        acc_reduce = acc_reduce + jnp.dot(hidden.T, go_vals, preferred_element_type=jnp.float32)
        acc_expand = acc_expand + jnp.dot(normed.T, dzvals, preferred_element_type=jnp.float32)
        grad = grad.reshape(BH, W, C)
        acc_dw = acc_dw + filter_grad(band, grad, BH, W)
        return ((acc_expand, acc_reduce, acc_dw), grad)
    init = (jnp.zeros((C, HID), jnp.float32), jnp.zeros((HID, C), jnp.float32), jnp.zeros((49, C), jnp.float32))
    sums, grads = lax.scan(band_step, init, jnp.arange(N_TY, dtype=jnp.int32))
    grad_full = grads.reshape(H, W, C)
    grad_pad = jnp.pad(grad_full, ((3, 3), (3, 3), (0, 0)))
    flipped = dw_weight[::-1]

    def out_step(carry, index):
        start = (index * BH).astype(jnp.int32)
        band = lax.dynamic_slice(grad_pad, (start, zero, zero), (BH + 6, W + 6, C))
        cot = lax.dynamic_slice(cotangent, (start, zero, zero), (BH, W, C))
        result = cot.astype(jnp.float32) + depthwise(band, flipped, BH, W)
        return (carry, result.astype(jnp.bfloat16))
    _, outs = lax.scan(out_step, jnp.float32(0.0), jnp.arange(N_TY, dtype=jnp.int32))
    grad_input = outs.reshape(H, W, C)
    factor = 1.0 / math.sqrt(H * W)
    return (grad_input, sums[2] * factor, sums[0] * factor, sums[1] * factor)
```

```python
import functools
import math

import jax
import jax.numpy as jnp
import numpy as np
from jax import lax
from jax.experimental import pallas as pl
from jax.experimental.pallas import tpu as pltpu
from jax.sharding import Mesh, PartitionSpec as P

F32, BF16 = jnp.float32, jnp.bfloat16
TILE = 16
LANES = 128
RG = 8
CB = 3
DW_ROWS = 32
VMEM = pl.BlockSpec(memory_space=pltpu.VMEM)
PARAMS = dict(vmem_limit_bytes=56 << 20)


def nn(a, b):
    return lax.dot_general(a, b, (((1,), (0,)), ((), ())), preferred_element_type=F32)


def nt(a, b):
    return lax.dot_general(a, b, (((1,), (1,)), ((), ())), preferred_element_type=F32)


def half(h):
    return slice(h * LANES, (h + 1) * LANES)


def spread_weights(w_ref, wide, flip):
    for h in range(2):
        for t in range(49):
            s = 48 - t if flip else t
            wide[h, t] = jnp.broadcast_to(w_ref[s : s + 1, half(h)], (8, LANES))


def fill(pad, core, top, bottom, left, right):
    rows, cols = core.shape[0], core.shape[1]
    for h in range(2):

        def put(i, _):
            pad[h, 3 + i, 8 : 8 + cols, :] = core[i, :, half(h)].astype(F32)
            return 0

        lax.fori_loop(0, rows, put, 0, unroll=4)
        for i in range(3):
            pad[h, i, 8 : 8 + cols, :] = top[i, :, half(h)].astype(F32)
            pad[h, 3 + rows + i, 8 : 8 + cols, :] = bottom[i, :, half(h)].astype(F32)
            for r in range(rows + 6):
                pad[h, r, 5 + i : 6 + i, :] = left[i, r : r + 1, half(h)].astype(F32)
                pad[h, r, 8 + cols + i : 9 + cols + i, :] = right[i, r : r + 1, half(h)].astype(F32)


def stencil(pad, wide, h, row, col):
    acc = [[None] * CB for _ in range(RG)]
    for b in range(7):
        w = [wide[h, a * 7 + b] for a in range(7)]
        for r in range(RG + 6):
            for c in range(CB):
                v = pad[h, row + r, pl.ds(col + c * 8 + 5 + b, 8), :]
                for a in range(7):
                    i = r - a
                    if 0 <= i < RG:
                        p = v * w[a]
                        acc[i][c] = p if acc[i][c] is None else acc[i][c] + p
    return acc


def branch_kernel(
    tissue, x_ref, top, bottom, left, right, cot, w_ref, bias, gain, shift, we, be, wr, scale,
    g_ref, acc_ref,
    pad, wide, u_ref, rstd_ref, normed, normed_t, go, go_t, hid, dz, dn,
):
    step = pl.program_id(0)
    rows, cols, chans = cot.shape
    pix = rows * cols
    hidden = we.shape[1]
    chunk = 256

    @pl.when(step == 0)
    def _():
        spread_weights(w_ref, wide, False)
        fill(pad, x_ref, top, bottom, left, right)
        acc_ref[...] = jnp.zeros_like(acc_ref)

    ng = cols // (8 * CB)
    for h in range(2):

        def conv(n, _):
            row, col = (n // ng) * RG, (n % ng) * (8 * CB)
            acc = stencil(pad, wide, h, step * rows + row, col)
            for i in range(RG):
                for c in range(CB):
                    at = pl.multiple_of((row + i) * cols + col + c * 8, 8)
                    u_ref[pl.ds(at, 8), half(h)] = acc[i][c] + bias[0:1, half(h)]
            return 0

        lax.fori_loop(0, (rows // RG) * ng, conv, 0)

    tiles = cols // TILE
    for c in range(tiles):
        keep = tissue[step, c].astype(F32)
        part = cot[:, c * TILE : (c + 1) * TILE, :].astype(F32) * (scale[0:1, :] * keep)
        for i in range(rows):
            go[i * cols + c * TILE : i * cols + (c + 1) * TILE, :] = part[i].astype(BF16)

    def norm(i, _):
        at = pl.ds(pl.multiple_of(i * cols, cols), cols)
        u = u_ref[at, :]
        center = u - jnp.sum(u, axis=-1, keepdims=True) * (1.0 / chans)
        var = jnp.sum(center * center, axis=-1, keepdims=True) * (1.0 / chans)
        rstd = lax.rsqrt(var + 1e-06)
        nhat = center * rstd
        u_ref[at, :] = nhat
        rstd_ref[at, :] = jnp.broadcast_to(rstd, (cols, LANES))
        normed[at, :] = (nhat * gain[0:1, :] + shift[0:1, :]).astype(BF16)
        return 0

    lax.fori_loop(0, rows, norm, 0, unroll=4)
    normed_t[...] = normed[...].T
    go_t[...] = go[...].T

    def mlp(k, _):
        at = pl.ds(pl.multiple_of(k * chunk, chunk), chunk)
        z = nn(normed[...], we[:, at]) + be[0:1, at]
        cdf = 0.5 * (1.0 + lax.erf(z * 0.7071067811865476))
        hid[...] = (z * cdf).astype(BF16)
        slope = cdf + z * jnp.exp(-0.5 * z * z) * 0.3989422804014327
        dz[...] = (nt(go[...], wr[at, :]) * slope).astype(BF16)
        part = nt(dz[...], we[:, at])
        @pl.when(k == 0)
        def _():
            dn[...] = part
        @pl.when(k > 0)
        def _():
            dn[...] += part
        acc_ref[0:chans, at] += nn(normed_t[...], dz[...])
        acc_ref[chans : 2 * chans, at] += nn(go_t[...], hid[...])
        return 0

    lax.fori_loop(0, hidden // chunk, mlp, 0)

    def back(i, _):
        at = pl.ds(pl.multiple_of(i * cols, cols), cols)
        nhat = u_ref[at, :]
        d = dn[at, :] * gain[0:1, :]
        first = jnp.sum(d, axis=-1, keepdims=True) * (1.0 / chans)
        second = jnp.sum(d * nhat, axis=-1, keepdims=True) * (1.0 / chans)
        rstd = rstd_ref[at, :]
        g = jnp.concatenate([rstd, rstd], axis=1) * (d - first - nhat * second)
        g_ref[i] = g.astype(BF16)
        return 0

    lax.fori_loop(0, rows, back, 0, unroll=4)


def branch(x, halo, cot, tissue, w, bias, gain, shift, we, be, wr, scale):
    rows, cols, chans = x.shape
    hidden = we.shape[1]
    pix = TILE * cols
    block = pl.BlockSpec((TILE, cols, chans), lambda s, t: (s, 0, 0))
    grid = pltpu.PrefetchScalarGridSpec(
        num_scalar_prefetch=1,
        grid=(rows // TILE,),
        in_specs=[VMEM] * 5 + [block] + [VMEM] * 8,
        out_specs=[block, pl.BlockSpec((2 * chans, hidden), lambda s, t: (0, 0))],
        scratch_shapes=[
            pltpu.VMEM((2, rows + 6, cols + 16, LANES), F32),
            pltpu.VMEM((2, 49, 8, LANES), F32),
            pltpu.VMEM((pix, chans), F32),
            pltpu.VMEM((pix, LANES), F32),
            pltpu.VMEM((pix, chans), BF16),
            pltpu.VMEM((chans, pix), BF16),
            pltpu.VMEM((pix, chans), BF16),
            pltpu.VMEM((chans, pix), BF16),
            pltpu.VMEM((pix, 256), BF16),
            pltpu.VMEM((pix, 256), BF16),
            pltpu.VMEM((pix, chans), F32),
        ],
    )
    return pl.pallas_call(
        branch_kernel,
        grid_spec=grid,
        out_shape=(
            jax.ShapeDtypeStruct(x.shape, BF16),
            jax.ShapeDtypeStruct((2 * chans, hidden), F32),
        ),
        compiler_params=pltpu.CompilerParams(**PARAMS),
        name="branch",
    )(tissue, x, *halo, cot, w, bias, gain, shift, we, be, wr, scale)


def filter_kernel(x_ref, top, bottom, left, right, g_ref, o_ref, pad, gpad):
    rows, cols, _ = g_ref.shape
    fill(pad, x_ref, top, bottom, left, right)
    o_ref[...] = jnp.zeros_like(o_ref)
    for h in range(2):
        for i in range(3):
            gpad[i] = jnp.zeros((cols, LANES), F32)
            gpad[rows + 3 + i] = jnp.zeros((cols, LANES), F32)

        def put(i, _):
            gpad[3 + i] = g_ref[i, :, half(h)].astype(F32)
            return 0

        lax.fori_loop(0, rows, put, 0, unroll=4)
        for first, count in ((0, 4), (4, 3)):

            def step(n, accs):
                r, col = first + n // (cols // 8), (n % (cols // 8)) * 8
                xs = [pad[h, r, pl.ds(col + 5 + b, 8), :] for b in range(7)]
                out = []
                for k in range(count):
                    g = gpad[r - (first + k) + 3, pl.ds(pl.multiple_of(col, 8), 8), :]
                    out += [accs[k * 7 + b] + xs[b] * g for b in range(7)]
                return tuple(out)

            zero = jnp.zeros((8, LANES), F32)
            accs = lax.fori_loop(
                0, (rows + count - 1) * (cols // 8), step, (zero,) * (7 * count), unroll=6
            )
            for k in range(count):
                for b in range(7):
                    t = (first + k) * 7 + b
                    at = (t % 4) * 256 + h * LANES
                    o_ref[t // 4 : t // 4 + 1, at : at + LANES] = jnp.sum(
                        accs[k * 7 + b], axis=0, keepdims=True
                    )


def filter_grad(x, halo, g):
    rows, cols, _ = x.shape
    return pl.pallas_call(
        filter_kernel,
        out_shape=jax.ShapeDtypeStruct((DW_ROWS, 1024), F32),
        in_specs=[VMEM] * 6,
        out_specs=VMEM,
        scratch_shapes=[
            pltpu.VMEM((2, rows + 6, cols + 16, LANES), F32),
            pltpu.VMEM((rows + 6, cols, LANES), F32),
        ],
        compiler_params=pltpu.CompilerParams(**PARAMS),
        name="filter_grad",
    )(x, *halo, g)


def input_kernel(g_ref, top, bottom, left, right, cot, w_ref, o_ref, pad, wide):
    rows, cols, _ = g_ref.shape
    spread_weights(w_ref, wide, True)
    fill(pad, g_ref, top, bottom, left, right)
    ng = cols // (8 * CB)
    for h in range(2):

        def step(n, _):
            row, col = (n // ng) * RG, (n % ng) * (8 * CB)
            acc = stencil(pad, wide, h, row, col)
            for i in range(RG):
                at = pl.ds(pl.multiple_of(col, 8), 8 * CB)
                value = jnp.concatenate(acc[i], axis=0)
                o_ref[row + i, at, half(h)] = (
                    cot[row + i, at, half(h)].astype(F32) + value
                ).astype(BF16)
            return 0

        lax.fori_loop(0, (rows // RG) * ng, step, 0)


def input_grad(g, halo, cot, w):
    rows, cols, _ = g.shape
    return pl.pallas_call(
        input_kernel,
        out_shape=jax.ShapeDtypeStruct(g.shape, BF16),
        in_specs=[VMEM] * 7,
        out_specs=VMEM,
        scratch_shapes=[
            pltpu.VMEM((2, rows + 6, cols + 16, LANES), F32),
            pltpu.VMEM((2, 49, 8, LANES), F32),
        ],
        compiler_params=pltpu.CompilerParams(**PARAMS),
        name="input_grad",
    )(g, *halo, cot, w)


def shifts(count):
    forward = [(i, i + 1) for i in range(count - 1)]
    return forward, [(b, a) for a, b in forward]


def halo_of(block, ty, tx, sizes):
    rows, cols = block.shape[:2]
    forward, backward = shifts(sizes[0])
    top = lax.ppermute(block[rows - 3 :], ty, forward)
    bottom = lax.ppermute(block[:3], ty, backward)

    def edge(at):
        parts = [p[:, at : at + 3].transpose(1, 0, 2) for p in (top, block, bottom)]
        return jnp.concatenate(parts, axis=1)

    forward, backward = shifts(sizes[1])
    left = lax.ppermute(edge(cols - 3), tx, forward)
    right = lax.ppermute(edge(0), tx, backward)
    return top, bottom, left, right


AXES = ("y", "x_hi", "core", "z", "x_lo")
SIZES = (4, 2, 2, 8, 2)
TY, TX = AXES[:3], AXES[3:]
PAIRS = ("core", "x_lo", "x_hi")
REST = ("y", "z")


def swap(value, axis):
    at = AXES.index(axis)
    index = np.arange(math.prod(SIZES)).reshape(SIZES)
    other = np.flip(index, axis=at)
    pairs = [(int(a), int(b)) for a, b in zip(index.ravel(), other.ravel())]
    return lax.ppermute(value, AXES, pairs)


def total(parts):
    parts = list(parts)
    rows = sum(p.shape[0] for p in parts)
    for axis in PAIRS:
        upper = lax.axis_index(axis) == 1
        width = parts[0].shape[1] // 2
        send = [jnp.where(upper, p[:, :width], p[:, width:]) for p in parts]
        got = swap(jnp.concatenate([s.astype(BF16) for s in send]), axis).astype(F32)
        kept, first = [], 0
        for p in parts:
            mine = jnp.where(upper, p[:, width:], p[:, :width])
            kept.append(mine + got[first : first + p.shape[0]])
            first += p.shape[0]
        parts = kept
    count = math.prod(SIZES[AXES.index(a)] for a in REST)
    whole = jnp.concatenate([p.astype(BF16) for p in parts])
    width = whole.shape[1]
    split = whole.reshape(count, rows // count, width)
    split = lax.all_to_all(split, REST, 0, 0, tiled=True)
    mine = jnp.sum(split.astype(F32), axis=0).astype(BF16)
    out = lax.all_to_all(jnp.broadcast_to(mine, split.shape), REST, 0, 0, tiled=True)
    out = out.reshape(rows, width)
    for axis in reversed(PAIRS):
        upper = lax.axis_index(axis) == 1
        got = swap(out, axis)
        low, high = jnp.where(upper, got, out), jnp.where(upper, out, got)
        out = jnp.concatenate([low, high], axis=1)
    return out


def body(x, cot, tissue, w, bias, gain, shift, we, be, wr, scale):
    rows, cols, chans = x.shape
    line = lambda v: v.reshape(1, -1)
    sizes = (math.prod(SIZES[:3]), math.prod(SIZES[3:]))
    factor = 1.0 / math.sqrt(rows * sizes[0] * cols * sizes[1])
    halo = halo_of(x, TY, TX, sizes)
    g, sums = branch(
        x, halo, cot, tissue, w, line(bias), line(gain), line(shift), we, line(be), wr, line(scale)
    )
    dw = filter_grad(x, halo, g)
    result = input_grad(g, halo_of(g, TY, TX, sizes), cot, w)
    out = total((sums, dw)).astype(F32) * factor
    taps = out[2 * chans :].reshape(-1, chans)[: w.shape[0]]
    return result, taps, out[:chans], out[chans : 2 * chans].T


def solution(mesh):
    fine = Mesh(mesh.devices.reshape(SIZES), AXES)
    pixels = P(TY, TX, None)
    return jax.shard_map(
        body,
        mesh=fine,
        in_specs=(pixels, pixels, P(TY, TX)) + (P(),) * 8,
        out_specs=(pixels, P(), P(), P()),
        check_vma=False,
    )
```

```python
import math

import jax
import jax.numpy as jnp
import numpy as np
from jax import lax
from jax.experimental import pallas as pl
from jax.experimental.pallas import tpu as pltpu
from jax.sharding import Mesh, PartitionSpec as P


F32, BF16 = jnp.float32, jnp.bfloat16
TILE = 16
LANES = 128
RG = 8
CB = 3
TAPS = 64
VMEM = pl.BlockSpec(memory_space=pltpu.VMEM)
PARAMS = dict(vmem_limit_bytes=56 << 20)


def nn(a, b):
    return lax.dot_general(a, b, (((1,), (0,)), ((), ())), preferred_element_type=F32)


def nt(a, b):
    return lax.dot_general(a, b, (((1,), (1,)), ((), ())), preferred_element_type=F32)


def half(h):
    return slice(h * LANES, (h + 1) * LANES)


def spread_weights(w_ref, wide, flip, halves=(0, 1)):
    for k, h in enumerate(halves):
        for t in range(49):
            s = 48 - t if flip else t
            wide[k, t] = jnp.broadcast_to(w_ref[s : s + 1, half(h)], (8, LANES))


def fill(pad, core, top, bottom, left, right, halves=(0, 1)):
    rows, cols = core.shape[0], core.shape[1]
    for k, h in enumerate(halves):

        def put(i, _):
            pad[k, 3 + i, 8 : 8 + cols, :] = core[i, :, half(h)].astype(F32)
            return 0

        lax.fori_loop(0, rows, put, 0, unroll=4)
        for i in range(3):
            pad[k, i, 8 : 8 + cols, :] = top[i, :, half(h)].astype(F32)
            pad[k, 3 + rows + i, 8 : 8 + cols, :] = bottom[i, :, half(h)].astype(F32)

        def side(first, count):
            for j in range(3):
                lv = left[j, pl.ds(first, count), half(h)].astype(F32)
                rv = right[j, pl.ds(first, count), half(h)].astype(F32)
                for r in range(count):
                    pad[k, first + r, 5 + j : 6 + j, :] = lv[r : r + 1]
                    pad[k, first + r, 8 + cols + j : 9 + cols + j, :] = rv[r : r + 1]

        def eight(i, _):
            side(i * 8, 8)
            return 0

        lax.fori_loop(0, (rows + 6) // 8, eight, 0)
        side((rows + 6) // 8 * 8, (rows + 6) % 8)


def stencil(pad, wide, h, row, col):
    acc = [[None] * CB for _ in range(RG)]
    for b in range(7):
        w = [wide[h, a * 7 + b] for a in range(7)]
        for r in range(RG + 6):
            for c in range(CB):
                v = pad[h, row + r, pl.ds(col + c * 8 + 5 + b, 8), :]
                for a in range(7):
                    i = r - a
                    if 0 <= i < RG:
                        p = v * w[a]
                        acc[i][c] = p if acc[i][c] is None else acc[i][c] + p
    return acc


def branch_kernel(
    tissue, x_ref, top, bottom, left, right, cot, w_ref, bias, gain, shift, we, be, wr, scale,
    g_ref, acc_ref,
    pad, wide, u_ref, nhat_ref, rstd_ref, normed, normed_t, go, go_t, hid, dz, dn,
):
    step = pl.program_id(0)
    rows, cols, chans = cot.shape
    hidden = we.shape[1]
    chunk = 256

    @pl.when(step == 0)
    def _():
        spread_weights(w_ref, wide, False)
        fill(pad, x_ref, top, bottom, left, right)
        acc_ref[...] = jnp.zeros_like(acc_ref)

    ng = cols // (8 * CB)
    for h in range(2):

        def conv(n, _):
            row, col = (n // ng) * RG, (n % ng) * (8 * CB)
            acc = stencil(pad, wide, h, step * rows + row, col)
            for i in range(RG):
                for c in range(CB):
                    at = pl.multiple_of((row + i) * cols + col + c * 8, 8)
                    u_ref[pl.ds(at, 8), half(h)] = acc[i][c] + bias[0:1, half(h)]
            return 0

        lax.fori_loop(0, (rows // RG) * ng, conv, 0)

    tiles = cols // TILE
    for c in range(tiles):
        keep = tissue[step, c].astype(F32)
        part = cot[:, c * TILE : (c + 1) * TILE, :].astype(F32) * (scale[0:1, :] * keep)
        for i in range(rows):
            go[i * cols + c * TILE : i * cols + (c + 1) * TILE, :] = part[i].astype(BF16)

    def norm(i, _):
        at = pl.ds(pl.multiple_of(i * cols, cols), cols)
        u = u_ref[at, :]
        center = u - jnp.sum(u, axis=-1, keepdims=True) * (1.0 / chans)
        var = jnp.sum(center * center, axis=-1, keepdims=True) * (1.0 / chans)
        rstd = lax.rsqrt(var + 1e-06)
        nhat = center * rstd
        nhat_ref[at, :] = nhat
        rstd_ref[at, :] = jnp.broadcast_to(rstd, (cols, LANES))
        normed[at, :] = (nhat * gain[0:1, :] + shift[0:1, :]).astype(BF16)
        return 0

    lax.fori_loop(0, rows, norm, 0, unroll=4)
    normed_t[...] = normed[...].T
    go_t[...] = go[...].T

    for k in range(hidden // chunk):
        at = slice(k * chunk, (k + 1) * chunk)
        z = nn(normed[...], we[:, at]) + be[0:1, at]
        cdf = 0.5 * (1.0 + lax.erf(z * 0.7071067811865476))
        hid[:, at] = (z * cdf).astype(BF16)
        slope = cdf + z * jnp.exp(-0.5 * z * z) * 0.3989422804014327
        dz[:, at] = (nt(go[...], wr[at, :]) * slope).astype(BF16)
    dn[...] = nt(dz[...], we[...])
    acc_ref[0:chans, :] += nn(normed_t[...], dz[...])
    acc_ref[chans : 2 * chans, :] += nn(go_t[...], hid[...])

    def back(i, _):
        at = pl.ds(pl.multiple_of(i * cols, cols), cols)
        nhat = nhat_ref[at, :]
        d = dn[at, :] * gain[0:1, :]
        first = jnp.sum(d, axis=-1, keepdims=True) * (1.0 / chans)
        second = jnp.sum(d * nhat, axis=-1, keepdims=True) * (1.0 / chans)
        rstd = rstd_ref[at, :]
        g = jnp.concatenate([rstd, rstd], axis=1) * (d - first - nhat * second)
        g_ref[i] = g.astype(BF16)
        return 0

    lax.fori_loop(0, rows, back, 0, unroll=4)


def branch(x, halo, cot, tissue, w, bias, gain, shift, we, be, wr, scale):
    rows, cols, chans = x.shape
    hidden = we.shape[1]
    pix = TILE * cols
    block = pl.BlockSpec((TILE, cols, chans), lambda s, t: (s, 0, 0))
    grid = pltpu.PrefetchScalarGridSpec(
        num_scalar_prefetch=1,
        grid=(rows // TILE,),
        in_specs=[VMEM] * 5 + [block] + [VMEM] * 8,
        out_specs=[block, pl.BlockSpec((2 * chans, hidden), lambda s, t: (0, 0))],
        scratch_shapes=[
            pltpu.VMEM((2, rows + 6, cols + 16, LANES), F32),
            pltpu.VMEM((2, 49, 8, LANES), F32),
            pltpu.VMEM((pix, chans), F32),
            pltpu.VMEM((pix, chans), F32),
            pltpu.VMEM((pix, LANES), F32),
            pltpu.VMEM((pix, chans), BF16),
            pltpu.VMEM((chans, pix), BF16),
            pltpu.VMEM((pix, chans), BF16),
            pltpu.VMEM((chans, pix), BF16),
            pltpu.VMEM((pix, hidden), BF16),
            pltpu.VMEM((pix, hidden), BF16),
            pltpu.VMEM((pix, chans), F32),
        ],
    )
    return pl.pallas_call(
        branch_kernel,
        grid_spec=grid,
        out_shape=(
            jax.ShapeDtypeStruct(x.shape, BF16),
            jax.ShapeDtypeStruct((2 * chans, hidden), F32),
        ),
        compiler_params=pltpu.CompilerParams(**PARAMS),
        cost_estimate=cost(32),
        name="branch",
    )(tissue, x, *halo, cot, w, bias, gain, shift, we, be, wr, scale)


def lane_half(shape, h):
    return pl.BlockSpec(shape[:-1] + (LANES,), lambda i, h=h: (0,) * (len(shape) - 1) + (h,))


def cost(us):
    return pl.CostEstimate(flops=0, transcendentals=0, bytes_accessed=int(us * 3.69e6))


def filter_kernel(x_ref, top, bottom, left, right, g_ref, o_ref, pad, gpad):
    rows, cols, _ = g_ref.shape
    fill(pad, x_ref, top, bottom, left, right, (0,))
    o_ref[...] = jnp.zeros_like(o_ref)
    for i in range(3):
        gpad[i] = jnp.zeros((cols, LANES), F32)
        gpad[rows + 3 + i] = jnp.zeros((cols, LANES), F32)

    def put(i, _):
        gpad[3 + i] = g_ref[i].astype(F32)
        return 0

    lax.fori_loop(0, rows, put, 0, unroll=4)
    for first, count in ((0, 4), (4, 3)):

        def step(n, accs):
            r = first + n // 2
            base = (n % 2) * (cols // 2)
            for c in range(cols // 16):
                xs = [pad[0, r, pl.ds(base + c * 8 + 5 + b, 8), :] for b in range(7)]
                out = []
                for k in range(count):
                    at = pl.ds(pl.multiple_of(base + c * 8, 8), 8)
                    g = gpad[r - (first + k) + 3, at, :]
                    out += [accs[k * 7 + b] + xs[b] * g for b in range(7)]
                accs = tuple(out)
            return accs

        zero = jnp.zeros((8, LANES), F32)
        accs = lax.fori_loop(0, (rows + count - 1) * 2, step, (zero,) * (7 * count), unroll=8)
        for k in range(count):
            for b in range(7):
                t = (first + k) * 7 + b
                o_ref[t : t + 1, :] = jnp.sum(accs[k * 7 + b], axis=0, keepdims=True)


def filter_grad(x, halo, g, h):
    rows, cols, _ = x.shape
    arrays = (x, *halo, g)
    return pl.pallas_call(
        filter_kernel,
        grid=(1,),
        out_shape=jax.ShapeDtypeStruct((TAPS, LANES), F32),
        in_specs=[lane_half(a.shape, h) for a in arrays],
        out_specs=pl.BlockSpec((TAPS, LANES), lambda i: (0, 0)),
        scratch_shapes=[
            pltpu.VMEM((1, rows + 6, cols + 16, LANES), F32),
            pltpu.VMEM((rows + 6, cols, LANES), F32),
        ],
        compiler_params=pltpu.CompilerParams(**PARAMS),
        cost_estimate=cost(7),
        name="filter_grad",
    )(*arrays)


def input_kernel(g_ref, top, bottom, left, right, cot, w_ref, o_ref, pad, wide, out):
    rows, cols, _ = g_ref.shape
    spread_weights(w_ref, wide, True, (0,))
    fill(pad, g_ref, top, bottom, left, right, (0,))
    ng = cols // (8 * CB)

    def step(n, _):
        row, col = (n // ng) * RG, (n % ng) * (8 * CB)
        acc = stencil(pad, wide, 0, row, col)
        for i in range(RG):
            for c in range(CB):
                at = pl.ds(pl.multiple_of(col + c * 8, 8), 8)
                out[row + i, at, :] = acc[i][c]
        return 0

    lax.fori_loop(0, (rows // RG) * ng, step, 0)

    def last(i, _):
        o_ref[i] = (cot[i].astype(F32) + out[i]).astype(BF16)
        return 0

    lax.fori_loop(0, rows, last, 0, unroll=4)


def input_grad(g, halo, cot, w, h):
    rows, cols, _ = g.shape
    arrays = (g, *halo, cot, w)
    return pl.pallas_call(
        input_kernel,
        grid=(1,),
        out_shape=jax.ShapeDtypeStruct((rows, cols, LANES), BF16),
        in_specs=[lane_half(a.shape, h) for a in arrays],
        out_specs=pl.BlockSpec((rows, cols, LANES), lambda i: (0, 0, 0)),
        scratch_shapes=[
            pltpu.VMEM((1, rows + 6, cols + 16, LANES), F32),
            pltpu.VMEM((1, 49, 8, LANES), F32),
            pltpu.VMEM((rows, cols, LANES), F32),
        ],
        compiler_params=pltpu.CompilerParams(**PARAMS),
        cost_estimate=cost(7),
        name="input_grad",
    )(*arrays)


def shifts(count):
    forward = [(i, i + 1) for i in range(count - 1)]
    return forward, [(b, a) for a, b in forward]


def halo_of(block, sizes):
    rows, cols = block.shape[:2]
    forward, backward = shifts(sizes[0])
    top = lax.ppermute(block[rows - 3 :], TY, forward)
    bottom = lax.ppermute(block[:3], TY, backward)

    def edge(at):
        parts = [p[:, at : at + 3].transpose(1, 0, 2) for p in (top, block, bottom)]
        return jnp.concatenate(parts, axis=1)

    forward, backward = shifts(sizes[1])
    left = lax.ppermute(edge(cols - 3), TX, forward)
    right = lax.ppermute(edge(0), TX, backward)
    return top, bottom, left, right


AXES = ("y", "x_hi", "core", "z", "x_lo")
SIZES = (4, 2, 2, 8, 2)
TY, TX = AXES[:3], AXES[3:]
PAIRS = ("core", "x_lo", "x_hi")
REST = ("y", "z")


def swap(value, axis):
    at = AXES.index(axis)
    index = np.arange(math.prod(SIZES)).reshape(SIZES)
    other = np.flip(index, axis=at)
    pairs = [(int(a), int(b)) for a, b in zip(index.ravel(), other.ravel())]
    return lax.ppermute(value, AXES, pairs)


def scatter(value):
    for axis in PAIRS:
        upper = lax.axis_index(axis) == 1
        width = value.shape[1] // 2
        low, high = value[:, :width], value[:, width:]
        got = swap(jnp.where(upper, low, high).astype(BF16), axis)
        value = jnp.where(upper, high, low) + got.astype(F32)
    return value


def exchange(value, taps):
    count = math.prod(SIZES[AXES.index(a)] for a in REST)
    blocks = [value.reshape(count, -1, LANES), taps.reshape(count, -1, LANES)]
    rows = blocks[0].shape[1]
    split = jnp.concatenate([b.astype(BF16) for b in blocks], axis=1)
    split = lax.all_to_all(split, REST, 0, 0, tiled=True)
    mine = jnp.sum(split.astype(F32), axis=0).astype(BF16)
    out = lax.all_to_all(jnp.broadcast_to(mine, split.shape), REST, 0, 0, tiled=True)
    return out[:, :rows].reshape(value.shape), out[:, rows:].reshape(taps.shape).astype(F32)


def gather(out, taps):
    shape = taps.shape
    for axis in reversed(PAIRS):
        upper = lax.axis_index(axis) == 1
        rows, width = out.shape
        sent = jnp.concatenate([out, taps.astype(BF16).reshape(-1, width)])
        got = swap(sent, axis)
        other = got[:rows]
        taps = taps + got[rows:].astype(F32).reshape(shape)
        out = jnp.concatenate([jnp.where(upper, other, out), jnp.where(upper, out, other)], axis=1)
    return out, taps


def body(x, cot, tissue, w, bias, gain, shift, we, be, wr, scale):
    rows, cols, chans = x.shape
    line = lambda v: v.reshape(1, -1)
    sizes = (math.prod(SIZES[:3]), math.prod(SIZES[3:]))
    factor = 1.0 / math.sqrt(rows * sizes[0] * cols * sizes[1])
    halo = halo_of(x, sizes)
    g, sums = branch(
        x, halo, cot, tissue, w, line(bias), line(gain), line(shift), we, line(be), wr, line(scale)
    )
    part = scatter(sums)
    taps = []
    for h in range(2):
        taps.append(filter_grad(x, halo, g, h))
    ghalo = halo_of(g, sizes)
    out, taps = exchange(part, jnp.concatenate(taps))
    result = []
    for h in range(2):
        result.append(input_grad(g, ghalo, cot, w, h))
    out, taps = gather(out, taps)
    out = out.astype(F32) * factor
    taps = (jnp.concatenate([taps[:TAPS], taps[TAPS:]], axis=1) * factor)[: w.shape[0]]
    return jnp.concatenate(result, axis=2), taps, out[:chans], out[chans:].T


def solution(mesh):
    fine = Mesh(mesh.devices.reshape(SIZES), AXES)
    pixels = P(TY, TX, None)
    return jax.shard_map(
        body,
        mesh=fine,
        in_specs=(pixels, pixels, P(TY, TX)) + (P(),) * 8,
        out_specs=(pixels, P(), P(), P()),
        check_vma=False,
    )
```

```python
import math

import jax
import jax.numpy as jnp
import numpy as np
from jax import lax
from jax.experimental import pallas as pl
from jax.experimental.pallas import tpu as pltpu
from jax.sharding import Mesh, PartitionSpec as P


F32, BF16 = jnp.float32, jnp.bfloat16
TILE = 16
LANES = 128
RG = 8
CB = 3
TAPS = 64
SPAN = 80
VMEM = pl.BlockSpec(memory_space=pltpu.VMEM)
PARAMS = dict(vmem_limit_bytes=56 << 20)


def nn(a, b):
    return lax.dot_general(a, b, (((1,), (0,)), ((), ())), preferred_element_type=F32)


def nt(a, b):
    return lax.dot_general(a, b, (((1,), (1,)), ((), ())), preferred_element_type=F32)


def half(h):
    return slice(h * LANES, (h + 1) * LANES)


def spread_weights(w_ref, wide, flip, halves=(0, 1)):
    for k, h in enumerate(halves):
        for t in range(49):
            s = 48 - t if flip else t
            wide[k, t] = jnp.broadcast_to(w_ref[s : s + 1, half(h)], (8, LANES))


def fill(pad, core, top, bottom, left, right, halves=(0, 1)):
    rows, cols = core.shape[0], core.shape[1]
    span = left.shape[0] // 3
    for k, h in enumerate(halves):

        def put(i, _):
            pad[k, 3 + i, 8 : 8 + cols, :] = core[i, :, half(h)].astype(F32)
            return 0

        lax.fori_loop(0, rows, put, 0, unroll=4)
        for i in range(3):
            pad[k, i, 8 : 8 + cols, :] = top[i * cols : (i + 1) * cols, half(h)].astype(F32)
            pad[k, 3 + rows + i, 8 : 8 + cols, :] = bottom[
                i * cols : (i + 1) * cols, half(h)
            ].astype(F32)

        def side(first, count):
            for j in range(3):
                at = pl.ds(pl.multiple_of(j * span + first, 8), 8)
                lv = left[at, half(h)].astype(F32)
                rv = right[at, half(h)].astype(F32)
                for r in range(count):
                    pad[k, first + r, 5 + j : 6 + j, :] = lv[r : r + 1]
                    pad[k, first + r, 8 + cols + j : 9 + cols + j, :] = rv[r : r + 1]

        def eight(i, _):
            side(i * 8, 8)
            return 0

        lax.fori_loop(0, (rows + 6) // 8, eight, 0)
        side((rows + 6) // 8 * 8, (rows + 6) % 8)


def stencil(pad, wide, h, row, col):
    acc = [[None] * CB for _ in range(RG)]
    for b in range(7):
        w = [wide[h, a * 7 + b] for a in range(7)]
        for r in range(RG + 6):
            for c in range(CB):
                v = pad[h, row + r, pl.ds(col + c * 8 + 5 + b, 8), :]
                for a in range(7):
                    i = r - a
                    if 0 <= i < RG:
                        p = v * w[a]
                        acc[i][c] = p if acc[i][c] is None else acc[i][c] + p
    return acc


def filter_sums(pad, gpad, taps):
    rows, cols = gpad.shape[1] - 6, gpad.shape[2]
    for h in range(2):
        for first, count in ((0, 4), (4, 3)):

            def step(n, accs):
                r = first + n // 2
                base = (n % 2) * (cols // 2)
                for c in range(cols // 16):
                    xs = [pad[h, r, pl.ds(base + c * 8 + 5 + b, 8), :] for b in range(7)]
                    out = []
                    for k in range(count):
                        at = pl.ds(pl.multiple_of(base + c * 8, 8), 8)
                        g = gpad[h, r - (first + k) + 3, at, :]
                        out += [accs[k * 7 + b] + xs[b] * g for b in range(7)]
                    accs = tuple(out)
                return accs

            zero = jnp.zeros((8, LANES), F32)
            accs = lax.fori_loop(0, (rows + count - 1) * 2, step, (zero,) * (7 * count), unroll=8)
            for k in range(count):
                for b in range(7):
                    t = h * TAPS + (first + k) * 7 + b
                    taps[t : t + 1, :] = jnp.sum(accs[k * 7 + b], axis=0, keepdims=True)
        taps[h * TAPS + 49 : (h + 1) * TAPS, :] = jnp.zeros((TAPS - 49, LANES), F32)


def branch_kernel(
    tissue, upper, x_ref, top, bottom, left, right, cot, w_ref, bias, gain, shift, we, be, wr, scale,
    g_ref, kept, sent, taps, acc_ref, gpad, pad, wide, u_ref, nhat_ref, rstd_ref, normed, normed_t, go, go_t, hid, dz, dn,
):
    step = pl.program_id(0)
    rows, cols, chans = cot.shape
    hidden = we.shape[1]
    chunk = 256

    @pl.when(step == 0)
    def _():
        spread_weights(w_ref, wide, False)
        fill(pad, x_ref, top, bottom, left, right)
        acc_ref[...] = jnp.zeros_like(acc_ref)
        for h in range(2):
            for i in range(3):
                gpad[h, i] = jnp.zeros((cols, LANES), F32)
                gpad[h, x_ref.shape[0] + 3 + i] = jnp.zeros((cols, LANES), F32)

    ng = cols // (8 * CB)
    for h in range(2):

        def conv(n, _):
            row, col = (n // ng) * RG, (n % ng) * (8 * CB)
            acc = stencil(pad, wide, h, step * rows + row, col)
            for i in range(RG):
                for c in range(CB):
                    at = pl.multiple_of((row + i) * cols + col + c * 8, 8)
                    u_ref[pl.ds(at, 8), half(h)] = acc[i][c] + bias[0:1, half(h)]
            return 0

        lax.fori_loop(0, (rows // RG) * ng, conv, 0)

    tiles = cols // TILE
    for c in range(tiles):
        keep = tissue[step, c].astype(F32)
        part = cot[:, c * TILE : (c + 1) * TILE, :].astype(F32) * (scale[0:1, :] * keep)
        for i in range(rows):
            go[i * cols + c * TILE : i * cols + (c + 1) * TILE, :] = part[i].astype(BF16)

    def norm(i, _):
        at = pl.ds(pl.multiple_of(i * cols, cols), cols)
        u = u_ref[at, :]
        center = u - jnp.sum(u, axis=-1, keepdims=True) * (1.0 / chans)
        var = jnp.sum(center * center, axis=-1, keepdims=True) * (1.0 / chans)
        rstd = lax.rsqrt(var + 1e-06)
        nhat = center * rstd
        nhat_ref[at, :] = nhat
        rstd_ref[at, :] = jnp.broadcast_to(rstd, (cols, LANES))
        normed[at, :] = (nhat * gain[0:1, :] + shift[0:1, :]).astype(BF16)
        return 0

    lax.fori_loop(0, rows, norm, 0, unroll=4)
    normed_t[...] = normed[...].T
    go_t[...] = go[...].T

    for k in range(hidden // chunk):
        at = slice(k * chunk, (k + 1) * chunk)
        z = nn(normed[...], we[:, at]) + be[0:1, at]
        cdf = 0.5 * (1.0 + lax.erf(z * 0.7071067811865476))
        hid[:, at] = (z * cdf).astype(BF16)
        slope = cdf + z * jnp.exp(-0.5 * z * z) * 0.3989422804014327
        dz[:, at] = (nt(go[...], wr[at, :]) * slope).astype(BF16)
    dn[...] = nt(dz[...], we[...])
    acc_ref[0:chans, :] += nn(normed_t[...], dz[...])
    acc_ref[chans : 2 * chans, :] += nn(go_t[...], hid[...])

    def back(i, _):
        at = pl.ds(pl.multiple_of(i * cols, cols), cols)
        nhat = nhat_ref[at, :]
        d = dn[at, :] * gain[0:1, :]
        first = jnp.sum(d, axis=-1, keepdims=True) * (1.0 / chans)
        second = jnp.sum(d * nhat, axis=-1, keepdims=True) * (1.0 / chans)
        rstd = rstd_ref[at, :]
        g = (jnp.concatenate([rstd, rstd], axis=1) * (d - first - nhat * second)).astype(BF16)
        g_ref[i] = g
        for h in range(2):
            gpad[h, step * rows + i + 3] = g[:, half(h)].astype(F32)
        return 0

    lax.fori_loop(0, rows, back, 0, unroll=4)

    @pl.when(step == pl.num_programs(0) - 1)
    def _():
        filter_sums(pad, gpad, taps)
        blocks = hidden // LANES
        side = upper[0]
        for e in range(blocks):
            cut = half(e)
            other = acc_ref[chans : 2 * chans, cut].T
            piece = [acc_ref[0:chans, cut], other[:, :LANES], other[:, LANES:]]
            piece = jnp.concatenate(piece, axis=0)
            size = piece.shape[0]
            at = pl.ds((e % (blocks // 2)) * size, size)
            mine = side == e // (blocks // 2)

            @pl.when(mine)
            def _(piece=piece, at=at):
                kept[at, :] = piece

            @pl.when(jnp.logical_not(mine))
            def _(piece=piece, at=at):
                sent[at, :] = piece.astype(BF16)


def branch(x, halo, cot, tissue, upper, w, bias, gain, shift, we, be, wr, scale):
    rows, cols, chans = x.shape
    hidden = we.shape[1]
    pix = TILE * cols
    block = pl.BlockSpec((TILE, cols, chans), lambda s, t, u: (s, 0, 0))
    whole = lambda *shape: pl.BlockSpec(shape, lambda s, t, u: (0, 0))
    size = 2 * chans * hidden // LANES // 2
    grid = pltpu.PrefetchScalarGridSpec(
        num_scalar_prefetch=2,
        grid=(rows // TILE,),
        in_specs=[VMEM] * 5 + [block] + [VMEM] * 8,
        out_specs=[block, whole(size, LANES), whole(size, LANES), whole(2 * TAPS, LANES)],
        scratch_shapes=[
            pltpu.VMEM((2 * chans, hidden), F32),
            pltpu.VMEM((2, rows + 6, cols, LANES), F32),
            pltpu.VMEM((2, rows + 6, cols + 16, LANES), F32),
            pltpu.VMEM((2, 49, 8, LANES), F32),
            pltpu.VMEM((pix, chans), F32),
            pltpu.VMEM((pix, chans), F32),
            pltpu.VMEM((pix, LANES), F32),
            pltpu.VMEM((pix, chans), BF16),
            pltpu.VMEM((chans, pix), BF16),
            pltpu.VMEM((pix, chans), BF16),
            pltpu.VMEM((chans, pix), BF16),
            pltpu.VMEM((pix, hidden), BF16),
            pltpu.VMEM((pix, hidden), BF16),
            pltpu.VMEM((pix, chans), F32),
        ],
    )
    return pl.pallas_call(
        branch_kernel,
        grid_spec=grid,
        out_shape=(
            jax.ShapeDtypeStruct(x.shape, BF16),
            jax.ShapeDtypeStruct((size, LANES), F32),
            jax.ShapeDtypeStruct((size, LANES), BF16),
            jax.ShapeDtypeStruct((2 * TAPS, LANES), F32),
        ),
        compiler_params=pltpu.CompilerParams(**PARAMS),
        cost_estimate=cost(42),
        name="branch",
    )(tissue, upper, x, *halo, cot, w, bias, gain, shift, we, be, wr, scale)


def cost(us):
    return pl.CostEstimate(flops=0, transcendentals=0, bytes_accessed=int(us * 3.69e6))


def input_kernel(g_ref, top, bottom, left, right, cot, w_ref, o_ref, pad, wide, out):
    step = pl.program_id(0)
    rows, cols, _ = cot.shape

    @pl.when(step == 0)
    def _():
        spread_weights(w_ref, wide, True, (0,))
        fill(pad, g_ref, top, bottom, left, right, (0,))

    ng = cols // (8 * CB)

    def conv(n, _):
        row, col = (n // ng) * RG, (n % ng) * (8 * CB)
        acc = stencil(pad, wide, 0, step * rows + row, col)
        for i in range(RG):
            for c in range(CB):
                at = pl.ds(pl.multiple_of(col + c * 8, 8), 8)
                out[row + i, at, :] = acc[i][c]
        return 0

    lax.fori_loop(0, (rows // RG) * ng, conv, 0)

    def last(i, _):
        o_ref[i] = (cot[i].astype(F32) + out[i]).astype(BF16)
        return 0

    lax.fori_loop(0, rows, last, 0, unroll=4)


def input_grad(g, halo, cot, w, h):
    rows, cols, _ = g.shape
    flat = lambda a: pl.BlockSpec((a.shape[0], LANES), lambda s, h=h: (0, h))
    block = pl.BlockSpec((TILE, cols, LANES), lambda s, h=h: (s, 0, h))
    return pl.pallas_call(
        input_kernel,
        grid=(rows // TILE,),
        out_shape=jax.ShapeDtypeStruct((rows, cols, LANES), BF16),
        in_specs=[pl.BlockSpec((rows, cols, LANES), lambda s, h=h: (0, 0, h))]
        + [flat(a) for a in halo]
        + [block, flat(w)],
        out_specs=pl.BlockSpec((TILE, cols, LANES), lambda s: (s, 0, 0)),
        scratch_shapes=[
            pltpu.VMEM((1, rows + 6, cols + 16, LANES), F32),
            pltpu.VMEM((1, 49, 8, LANES), F32),
            pltpu.VMEM((TILE, cols, LANES), F32),
        ],
        compiler_params=pltpu.CompilerParams(**PARAMS),
        cost_estimate=cost(7),
        name="input_grad",
    )(g, *halo, cot, w)


def shifts(count):
    forward = [(i, i + 1) for i in range(count - 1)]
    return forward, [(b, a) for a, b in forward]


def halo_of(block, sizes):
    rows, cols, chans = block.shape
    forward, backward = shifts(sizes[0])
    top = lax.ppermute(block[rows - 3 :].reshape(-1, chans), TY, forward)
    bottom = lax.ppermute(block[:3].reshape(-1, chans), TY, backward)

    def edge(at):
        parts = []
        for j in range(3):
            column = lambda flat: [flat[i * cols + at + j][None] for i in range(3)]
            parts += column(top) + [block[:, at + j]] + column(bottom)
            parts.append(jnp.zeros((SPAN - rows - 6, chans), BF16))
        return jnp.concatenate(parts)

    forward, backward = shifts(sizes[1])
    left = lax.ppermute(edge(cols - 3), TX, forward)
    right = lax.ppermute(edge(0), TX, backward)
    return top, bottom, left, right


AXES = ("y", "x_hi", "core", "z", "x_lo")
SIZES = (4, 2, 2, 8, 2)
TY, TX = AXES[:3], AXES[3:]
PAIRS = ("core", "x_lo", "x_hi")
REST = ("y", "z")


def swap(value, axis):
    at = AXES.index(axis)
    index = np.arange(math.prod(SIZES)).reshape(SIZES)
    other = np.flip(index, axis=at)
    pairs = [(int(a), int(b)) for a, b in zip(index.ravel(), other.ravel())]
    return lax.ppermute(value, AXES, pairs)


def scatter(kept, sent):
    for n, axis in enumerate(PAIRS):
        kept = kept + swap(sent, axis).astype(F32)
        if n + 1 < len(PAIRS):
            upper = lax.axis_index(PAIRS[n + 1]) == 1
            size = kept.shape[0] // 2
            low, high = kept[:size], kept[size:]
            sent = jnp.where(upper, low, high).astype(BF16)
            kept = jnp.where(upper, high, low)
    return kept


def exchange(value, taps):
    count = math.prod(SIZES[AXES.index(a)] for a in REST)
    blocks = [value.reshape(count, -1, LANES), taps.reshape(count, -1, LANES)]
    rows = blocks[0].shape[1]
    split = jnp.concatenate([b.astype(BF16) for b in blocks], axis=1)
    split = lax.all_to_all(split, REST, 0, 0, tiled=True)
    mine = jnp.sum(split.astype(F32), axis=0).astype(BF16)
    out = lax.all_to_all(jnp.broadcast_to(mine, split.shape), REST, 0, 0, tiled=True)
    return out[:, :rows].reshape(value.shape), out[:, rows:].reshape(taps.shape).astype(F32)


def gather(out, taps):
    for axis in reversed(PAIRS):
        upper = lax.axis_index(axis) == 1
        rows = out.shape[0]
        got = swap(jnp.concatenate([out, taps.astype(BF16)]), axis)
        other = got[:rows]
        taps = taps + got[rows:].astype(F32)
        out = jnp.concatenate([jnp.where(upper, other, out), jnp.where(upper, out, other)])
    return out, taps


def body(x, cot, tissue, w, bias, gain, shift, we, be, wr, scale):
    rows, cols, chans = x.shape
    line = lambda v: v.reshape(1, -1)
    sizes = (math.prod(SIZES[:3]), math.prod(SIZES[3:]))
    factor = 1.0 / math.sqrt(rows * sizes[0] * cols * sizes[1])
    halo = halo_of(x, sizes)
    upper = lax.axis_index(PAIRS[0]).astype(jnp.int32).reshape(1)
    rest = (w, line(bias), line(gain), line(shift), we, line(be), wr, line(scale))
    g, kept, sent, taps = branch(x, halo, cot, tissue, upper, *rest)
    ghalo = halo_of(g, sizes)
    out, taps = exchange(scatter(kept, sent), taps)
    result = []
    for h in range(2):
        result.append(input_grad(g, ghalo, cot, w, h))
    out, taps = gather(out, taps)
    out = out.reshape(-1, 2 * chans, LANES)
    expand = out[:, :chans].transpose(1, 0, 2).reshape(chans, -1)
    reduce = out[:, chans:].reshape(-1, 2, LANES, LANES).transpose(0, 2, 1, 3).reshape(-1, chans)
    taps = jnp.concatenate([taps[:TAPS], taps[TAPS:]], axis=1)[: w.shape[0]]
    scaled = [v.astype(F32) * factor for v in (taps, expand, reduce)]
    return (jnp.concatenate(result, axis=2), *scaled)


def solution(mesh):
    fine = Mesh(mesh.devices.reshape(SIZES), AXES)
    pixels = P(TY, TX, None)
    return jax.shard_map(
        body,
        mesh=fine,
        in_specs=(pixels, pixels, P(TY, TX)) + (P(),) * 8,
        out_specs=(pixels, P(), P(), P()),
        check_vma=False,
    )
```

```python
import math

import jax
import jax.numpy as jnp
import numpy as np
from jax import lax
from jax.experimental import pallas as pl
from jax.experimental.pallas import tpu as pltpu
from jax.sharding import Mesh, PartitionSpec as P


F32, BF16 = jnp.float32, jnp.bfloat16
TILE = 16
LANES = 128
RG = 8
CB = 3
TAPS = 64
EXTRA = 32
VMEM = pl.BlockSpec(memory_space=pltpu.VMEM)
PARAMS = dict(vmem_limit_bytes=56 << 20)


def nn(a, b):
    return lax.dot_general(a, b, (((1,), (0,)), ((), ())), preferred_element_type=F32)


def nt(a, b):
    return lax.dot_general(a, b, (((1,), (1,)), ((), ())), preferred_element_type=F32)


def half(h):
    return slice(h * LANES, (h + 1) * LANES)


def spread_weights(w_ref, wide, flip, halves=(0, 1)):
    for k, h in enumerate(halves):
        for t in range(49):
            s = 48 - t if flip else t
            wide[k, t] = jnp.broadcast_to(w_ref[s : s + 1, half(h)], (8, LANES))


def fill(pad, core, top, bottom, left, right, halves=(0, 1)):
    rows, cols = core.shape[0], core.shape[1]
    ends = (5, 8 + cols)
    for k, h in enumerate(halves):

        def put(i, _):
            pad[k, 3 + i, 8 : 8 + cols, :] = core[i, :, half(h)].astype(F32)
            return 0

        lax.fori_loop(0, rows, put, 0, unroll=4)
        for first, flat in ((0, top), (3 + rows, bottom)):
            extra = flat[3 * cols : 3 * cols + 24, half(h)].astype(F32)
            for i in range(3):
                at = slice(i * cols, (i + 1) * cols)
                pad[k, first + i, 8 : 8 + cols, :] = flat[at, half(h)].astype(F32)
                for n, end in enumerate(ends):
                    corner = extra[n * 9 + i * 3 : n * 9 + i * 3 + 3]
                    pad[k, first + i, end : end + 3, :] = corner

        def side(i, _):
            at = pl.ds(pl.multiple_of(i * 24, 8), 24)
            for end, flat in zip(ends, (left, right)):
                v = flat[at, half(h)].astype(F32)
                for r in range(8):
                    pad[k, 3 + i * 8 + r, end : end + 3, :] = v[r * 3 : r * 3 + 3]
            return 0

        lax.fori_loop(0, rows // 8, side, 0)


def stencil(pad, wide, h, row, col):
    acc = [[None] * CB for _ in range(RG)]
    for b in range(7):
        w = [wide[h, a * 7 + b] for a in range(7)]
        for r in range(RG + 6):
            for c in range(CB):
                v = pad[h, row + r, pl.ds(col + c * 8 + 5 + b, 8), :]
                for a in range(7):
                    i = r - a
                    if 0 <= i < RG:
                        p = v * w[a]
                        acc[i][c] = p if acc[i][c] is None else acc[i][c] + p
    return acc


def filter_sums(pad, gpad, taps):
    rows, cols = gpad.shape[1] - 6, gpad.shape[2]
    for h in range(2):
        for first, count in ((0, 4), (4, 3)):

            def step(n, accs):
                r = first + n // 2
                base = (n % 2) * (cols // 2)
                for c in range(cols // 16):
                    xs = [pad[h, r, pl.ds(base + c * 8 + 5 + b, 8), :] for b in range(7)]
                    out = []
                    for k in range(count):
                        at = pl.ds(pl.multiple_of(base + c * 8, 8), 8)
                        g = gpad[h, r - (first + k) + 3, at, :]
                        out += [accs[k * 7 + b] + xs[b] * g for b in range(7)]
                    accs = tuple(out)
                return accs

            zero = jnp.zeros((8, LANES), F32)
            accs = lax.fori_loop(0, (rows + count - 1) * 2, step, (zero,) * (7 * count), unroll=8)
            for k in range(count):
                for b in range(7):
                    t = h * TAPS + (first + k) * 7 + b
                    taps[t : t + 1, :] = jnp.sum(accs[k * 7 + b], axis=0, keepdims=True)
        taps[h * TAPS + 49 : (h + 1) * TAPS, :] = jnp.zeros((TAPS - 49, LANES), F32)


def branch_kernel(
    tissue, upper, x_ref, top, bottom, left, right, cot, w_ref, bias, gain, shift, we, be, wr, scale,
    g_ref, g_left, g_right, g_top, g_bottom, kept, sent, taps, acc_ref, gpad, pad, wide, u_ref, nhat_ref, rstd_ref, normed, normed_t, go, go_t, hid, dz, dn,
):
    step = pl.program_id(0)
    rows, cols, chans = cot.shape
    hidden = we.shape[1]
    chunk = 256

    @pl.when(step == 0)
    def _():
        spread_weights(w_ref, wide, False)
        fill(pad, x_ref, top, bottom, left, right)
        acc_ref[...] = jnp.zeros_like(acc_ref)
        for h in range(2):
            for i in range(3):
                gpad[h, i] = jnp.zeros((cols, LANES), F32)
                gpad[h, x_ref.shape[0] + 3 + i] = jnp.zeros((cols, LANES), F32)

    ng = cols // (8 * CB)
    for h in range(2):

        def conv(n, _):
            row, col = (n // ng) * RG, (n % ng) * (8 * CB)
            acc = stencil(pad, wide, h, step * rows + row, col)
            for i in range(RG):
                for c in range(CB):
                    at = pl.multiple_of((row + i) * cols + col + c * 8, 8)
                    u_ref[pl.ds(at, 8), half(h)] = acc[i][c] + bias[0:1, half(h)]
            return 0

        lax.fori_loop(0, (rows // RG) * ng, conv, 0)

    tiles = cols // TILE
    for c in range(tiles):
        keep = tissue[step, c].astype(F32)
        part = cot[:, c * TILE : (c + 1) * TILE, :].astype(F32) * (scale[0:1, :] * keep)
        for i in range(rows):
            go[i * cols + c * TILE : i * cols + (c + 1) * TILE, :] = part[i].astype(BF16)

    def norm(i, _):
        at = pl.ds(pl.multiple_of(i * cols, cols), cols)
        u = u_ref[at, :]
        center = u - jnp.sum(u, axis=-1, keepdims=True) * (1.0 / chans)
        var = jnp.sum(center * center, axis=-1, keepdims=True) * (1.0 / chans)
        rstd = lax.rsqrt(var + 1e-06)
        nhat = center * rstd
        nhat_ref[at, :] = nhat
        rstd_ref[at, :] = jnp.broadcast_to(rstd, (cols, LANES))
        normed[at, :] = (nhat * gain[0:1, :] + shift[0:1, :]).astype(BF16)
        return 0

    lax.fori_loop(0, rows, norm, 0, unroll=4)
    normed_t[...] = normed[...].T
    go_t[...] = go[...].T

    for k in range(hidden // chunk):
        at = slice(k * chunk, (k + 1) * chunk)
        z = nn(normed[...], we[:, at]) + be[0:1, at]
        cdf = 0.5 * (1.0 + lax.erf(z * 0.7071067811865476))
        hid[:, at] = (z * cdf).astype(BF16)
        slope = cdf + z * jnp.exp(-0.5 * z * z) * 0.3989422804014327
        dz[:, at] = (nt(go[...], wr[at, :]) * slope).astype(BF16)
    dn[...] = nt(dz[...], we[...])
    acc_ref[0:chans, :] += nn(normed_t[...], dz[...])
    acc_ref[chans : 2 * chans, :] += nn(go_t[...], hid[...])

    def back(i, _):
        at = pl.ds(pl.multiple_of(i * cols, cols), cols)
        nhat = nhat_ref[at, :]
        d = dn[at, :] * gain[0:1, :]
        first = jnp.sum(d, axis=-1, keepdims=True) * (1.0 / chans)
        second = jnp.sum(d * nhat, axis=-1, keepdims=True) * (1.0 / chans)
        rstd = rstd_ref[at, :]
        g = (jnp.concatenate([rstd, rstd], axis=1) * (d - first - nhat * second)).astype(BF16)
        g_ref[i] = g
        for h in range(2):
            gpad[h, step * rows + i + 3] = g[:, half(h)].astype(F32)
        return 0

    lax.fori_loop(0, rows, back, 0, unroll=4)

    @pl.when(step == pl.num_programs(0) - 1)
    def _():
        filter_sums(pad, gpad, taps)
        high = gpad.shape[1] - 6
        for h in range(2):
            for first, flat in ((3, g_top), (high, g_bottom)):
                for i in range(3):
                    flat[i * cols : (i + 1) * cols, half(h)] = gpad[h, first + i].astype(BF16)
            for col, flat in ((0, g_left), (cols - 3, g_right)):

                def collect(i, _, col=col, flat=flat, h=h):
                    v = [gpad[h, 3 + i * 16 + r, col : col + 3, :] for r in range(16)]
                    at = pl.ds(pl.multiple_of(i * 48, 16), 48)
                    flat[at, half(h)] = jnp.concatenate(v, axis=0).astype(BF16)
                    return 0

                lax.fori_loop(0, high // 16, collect, 0)
        blocks = hidden // LANES
        side = upper[0]
        for e in range(blocks):
            cut = half(e)
            other = acc_ref[chans : 2 * chans, cut].T
            count = 2 * TAPS // blocks
            piece = [acc_ref[0:chans, cut], other[:, :LANES], other[:, LANES:]]
            piece += [taps[e * count : (e + 1) * count, :], jnp.zeros((EXTRA - count, LANES), F32)]
            piece = jnp.concatenate(piece, axis=0)
            size = piece.shape[0]
            at = pl.ds((e % (blocks // 2)) * size, size)
            mine = side == e // (blocks // 2)

            @pl.when(mine)
            def _(piece=piece, at=at):
                kept[at, :] = piece

            @pl.when(jnp.logical_not(mine))
            def _(piece=piece, at=at):
                sent[at, :] = piece.astype(BF16)


def branch(x, halo, cot, tissue, upper, w, bias, gain, shift, we, be, wr, scale):
    rows, cols, chans = x.shape
    hidden = we.shape[1]
    pix = TILE * cols
    block = pl.BlockSpec((TILE, cols, chans), lambda s, t, u: (s, 0, 0))
    whole = lambda *shape: pl.BlockSpec(shape, lambda s, t, u: (0, 0))
    size = (2 * chans + EXTRA) * (hidden // LANES) // 2
    grid = pltpu.PrefetchScalarGridSpec(
        num_scalar_prefetch=2,
        grid=(rows // TILE,),
        in_specs=[VMEM] * 5 + [block] + [VMEM] * 8,
        out_specs=[block]
        + [whole(3 * rows, chans)] * 2
        + [whole(3 * cols, chans)] * 2
        + [whole(size, LANES)] * 2,
        scratch_shapes=[
            pltpu.VMEM((2 * TAPS, LANES), F32),
            pltpu.VMEM((2 * chans, hidden), F32),
            pltpu.VMEM((2, rows + 6, cols, LANES), F32),
            pltpu.VMEM((2, rows + 6, cols + 16, LANES), F32),
            pltpu.VMEM((2, 49, 8, LANES), F32),
            pltpu.VMEM((pix, chans), F32),
            pltpu.VMEM((pix, chans), F32),
            pltpu.VMEM((pix, LANES), F32),
            pltpu.VMEM((pix, chans), BF16),
            pltpu.VMEM((chans, pix), BF16),
            pltpu.VMEM((pix, chans), BF16),
            pltpu.VMEM((chans, pix), BF16),
            pltpu.VMEM((pix, hidden), BF16),
            pltpu.VMEM((pix, hidden), BF16),
            pltpu.VMEM((pix, chans), F32),
        ],
    )
    return pl.pallas_call(
        branch_kernel,
        grid_spec=grid,
        out_shape=(
            jax.ShapeDtypeStruct(x.shape, BF16),
            jax.ShapeDtypeStruct((3 * rows, chans), BF16),
            jax.ShapeDtypeStruct((3 * rows, chans), BF16),
            jax.ShapeDtypeStruct((3 * cols, chans), BF16),
            jax.ShapeDtypeStruct((3 * cols, chans), BF16),
            jax.ShapeDtypeStruct((size, LANES), F32),
            jax.ShapeDtypeStruct((size, LANES), BF16),
        ),
        compiler_params=pltpu.CompilerParams(**PARAMS),
        cost_estimate=cost(42),
        name="branch",
    )(tissue, upper, x, *halo, cot, w, bias, gain, shift, we, be, wr, scale)


def cost(us):
    return pl.CostEstimate(flops=0, transcendentals=0, bytes_accessed=int(us * 3.69e6))


def input_kernel(g_ref, top, bottom, left, right, cot, w_ref, o_ref, pad, wide, out):
    step = pl.program_id(0)
    rows, cols, _ = cot.shape

    @pl.when(step == 0)
    def _():
        spread_weights(w_ref, wide, True, (0,))
        fill(pad, g_ref, top, bottom, left, right, (0,))

    ng = cols // (8 * CB)

    def conv(n, _):
        row, col = (n // ng) * RG, (n % ng) * (8 * CB)
        acc = stencil(pad, wide, 0, step * rows + row, col)
        for i in range(RG):
            for c in range(CB):
                at = pl.ds(pl.multiple_of(col + c * 8, 8), 8)
                out[row + i, at, :] = acc[i][c]
        return 0

    lax.fori_loop(0, (rows // RG) * ng, conv, 0)

    def last(i, _):
        o_ref[i] = (cot[i].astype(F32) + out[i]).astype(BF16)
        return 0

    lax.fori_loop(0, rows, last, 0, unroll=4)


def input_grad(g, halo, cot, w, h):
    rows, cols, _ = g.shape
    flat = lambda a: pl.BlockSpec((a.shape[0], LANES), lambda s, h=h: (0, h))
    block = pl.BlockSpec((TILE, cols, LANES), lambda s, h=h: (s, 0, h))
    return pl.pallas_call(
        input_kernel,
        grid=(rows // TILE,),
        out_shape=jax.ShapeDtypeStruct((rows, cols, LANES), BF16),
        in_specs=[pl.BlockSpec((rows, cols, LANES), lambda s, h=h: (0, 0, h))]
        + [flat(a) for a in halo]
        + [block, flat(w)],
        out_specs=pl.BlockSpec((TILE, cols, LANES), lambda s: (s, 0, 0)),
        scratch_shapes=[
            pltpu.VMEM((1, rows + 6, cols + 16, LANES), F32),
            pltpu.VMEM((1, 49, 8, LANES), F32),
            pltpu.VMEM((TILE, cols, LANES), F32),
        ],
        compiler_params=pltpu.CompilerParams(**PARAMS),
        cost_estimate=cost(7),
        name="input_grad",
    )(g, *halo, cot, w)


AXES = ("y", "x_hi", "core", "z", "x_lo")
SIZES = (4, 2, 2, 8, 2)
TY, TX = AXES[:3], AXES[3:]


def beside(value, axes, odd):
    count = math.prod(SIZES[AXES.index(a)] for a in axes)
    pairs = [(i, i + 1) for i in range(odd, count - 1, 2)]
    return lax.ppermute(value, axes, pairs + [(b, a) for a, b in pairs])


def both_sides(low, high, axes):
    odd = lax.axis_index(axes) % 2 == 1
    first = beside(jnp.where(odd, low, high), axes, 0)
    second = beside(jnp.where(odd, high, low), axes, 1)
    return jnp.where(odd, first, second), jnp.where(odd, second, first)


def halo_of(left, right, top, bottom):
    chans = left.shape[1]
    left, right = both_sides(left, right, TX)
    filler = jnp.zeros((14, chans), BF16)
    top = jnp.concatenate([top, left[:9], right[:9], filler])
    bottom = jnp.concatenate([bottom, left[-9:], right[-9:], filler])
    top, bottom = both_sides(top, bottom, TY)
    return top, bottom, left, right


SWAPS = {
    "core": (("core",), ("core",)),
    "x_near": (("x_lo",), ("x_lo", "x_hi")),
    "x_far": (("x_lo", "x_hi"), ("x_hi",)),
    "y_near": ((("y", 1),), (("y", 1), ("y", 2))),
    "y_far": ((("y", 3),), (("y", 2),)),
}


def keeps_upper(name):
    bit = 0
    for item in SWAPS[name][1]:
        axis, mask = item if isinstance(item, tuple) else (item, 1)
        bit = bit + (lax.axis_index(axis) // mask) % 2
    return bit % 2


def swap(value, name):
    index = np.arange(math.prod(SIZES)).reshape(SIZES)
    where = np.indices(SIZES)
    for item in SWAPS[name][0]:
        axis, mask = item if isinstance(item, tuple) else (item, 1)
        where[AXES.index(axis)] ^= mask
    other = index[tuple(where)]
    pairs = [(int(a), int(b)) for a, b in zip(index.ravel(), other.ravel())]
    return lax.ppermute(value, AXES, pairs)


def total(kept, sent):
    names = list(SWAPS)
    for n, name in enumerate(names):
        kept = kept + swap(sent, name).astype(F32)
        if n + 1 < len(names):
            upper = keeps_upper(names[n + 1]) == 1
            size = kept.shape[0] // 2
            low, high = kept[:size], kept[size:]
            sent = jnp.where(upper, low, high).astype(BF16)
            kept = jnp.where(upper, high, low)
    count = SIZES[AXES.index("z")]
    copies = jnp.broadcast_to(kept.astype(BF16)[None], (count, *kept.shape))
    copies = lax.all_to_all(copies, "z", 0, 0, tiled=True)
    out = jnp.sum(copies.astype(F32), axis=0).astype(BF16)
    for name in reversed(names):
        upper = keeps_upper(name) == 1
        other = swap(out, name)
        out = jnp.concatenate([jnp.where(upper, other, out), jnp.where(upper, out, other)])
    return out


def body(x, cot, tissue, w, bias, gain, shift, we, be, wr, scale):
    rows, cols, chans = x.shape
    line = lambda v: v.reshape(1, -1)
    sizes = (math.prod(SIZES[:3]), math.prod(SIZES[3:]))
    factor = 1.0 / math.sqrt(rows * sizes[0] * cols * sizes[1])
    edges = (x[:, :3], x[:, cols - 3 :], x[:3], x[rows - 3 :])
    halo = halo_of(*(v.reshape(-1, chans) for v in edges))
    upper = keeps_upper("core").astype(jnp.int32).reshape(1)
    rest = (w, line(bias), line(gain), line(shift), we, line(be), wr, line(scale))
    g, *edges, kept, sent = branch(x, halo, cot, tissue, upper, *rest)
    ghalo = halo_of(*edges)
    result = []
    for h in range(2):
        result.append(input_grad(g, ghalo, cot, w, h))
    out = total(kept, sent).reshape(-1, 2 * chans + EXTRA, LANES)
    expand = out[:, :chans].transpose(1, 0, 2).reshape(chans, -1)
    reduce = out[:, chans : 2 * chans].reshape(-1, 2, LANES, LANES)
    reduce = reduce.transpose(0, 2, 1, 3).reshape(-1, chans)
    taps = out[:, 2 * chans : 2 * chans + 2 * TAPS // out.shape[0]].reshape(2, TAPS, LANES)
    taps = taps.transpose(1, 0, 2).reshape(TAPS, chans)[: w.shape[0]]
    scaled = [v.astype(F32) * factor for v in (taps, expand, reduce)]
    return (jnp.concatenate(result, axis=2), *scaled)


def solution(mesh):
    fine = Mesh(mesh.devices.reshape(SIZES), AXES)
    pixels = P(TY, TX, None)
    return jax.shard_map(
        body,
        mesh=fine,
        in_specs=(pixels, pixels, P(TY, TX)) + (P(),) * 8,
        out_specs=(pixels, P(), P(), P()),
        check_vma=False,
    )
```

```python
import functools
import math

import jax
import jax.numpy as jnp
import numpy as np
from jax import lax
from jax.experimental import pallas as pl
from jax.experimental.pallas import tpu as pltpu
from jax.sharding import Mesh, PartitionSpec as P


F32, BF16 = jnp.float32, jnp.bfloat16
TILE = 16
LANES = 128
RG = 8
CB = 3
TAPS = 64
PART = 16
EXTRA = 32
VMEM = pl.BlockSpec(memory_space=pltpu.VMEM)


def nn(a, b):
    return lax.dot_general(a, b, (((1,), (0,)), ((), ())), preferred_element_type=F32)


def nt(a, b):
    return lax.dot_general(a, b, (((1,), (1,)), ((), ())), preferred_element_type=F32)


def half(h):
    return slice(h * LANES, (h + 1) * LANES)


def spread_weights(w_ref, wide, flip, halves=(0, 1)):
    for k, h in enumerate(halves):
        for t in range(49):
            s = 48 - t if flip else t
            wide[k, t] = jnp.broadcast_to(w_ref[s : s + 1, half(h)], (8, LANES))


def fill(pad, core, top, bottom, left, right, base=0, count=None):
    rows, cols = core.shape[0], core.shape[1]
    count = rows if count is None else count
    ends = (5, 8 + cols)
    first, stop = max(base - 3, 0), min(base + count + 3, rows)
    edges = []
    if base == 0:
        edges.append((0, top))
    if base + count == rows:
        edges.append((3 + count, bottom))
    for h in range(2):

        def put(i, _):
            pad[h, i - base + 3, 8 : 8 + cols, :] = core[i, :, half(h)].astype(F32)
            return 0

        lax.fori_loop(first, stop, put, 0, unroll=4 if (stop - first) % 4 == 0 else 1)
        for at, flat in edges:
            extra = flat[3 * cols : 3 * cols + 24, half(h)].astype(F32)
            for i in range(3):
                line = flat[i * cols : (i + 1) * cols, half(h)].astype(F32)
                pad[h, at + i, 8 : 8 + cols, :] = line
                for n, end in enumerate(ends):
                    corner = extra[n * 9 + i * 3 : n * 9 + i * 3 + 3]
                    pad[h, at + i, end : end + 3, :] = corner

        def side(start, lines):
            at = pl.ds(pl.multiple_of(start * 3, 8), 24)
            for end, flat in zip(ends, (left, right)):
                v = flat[at, half(h)].astype(F32)
                for r in lines:
                    pad[h, 3 - base + start + r, end : end + 3, :] = v[r * 3 : r * 3 + 3]

        def eight(i, _):
            side(base + i * 8, range(8))
            return 0

        lax.fori_loop(0, count // 8, eight, 0)
        if first < base:
            side(base - 8, range(8 - (base - first), 8))
        if stop > base + count:
            side(base + count, range(stop - base - count))


def stencil(pad, wide, h, row, col):
    acc = [[None] * CB for _ in range(RG)]
    for b in range(7):
        w = [wide[h, a * 7 + b] for a in range(7)]
        for r in range(RG + 6):
            for c in range(CB):
                v = pad[h, row + r, pl.ds(col + c * 8 + 5 + b, 8), :]
                for a in range(7):
                    i = r - a
                    if 0 <= i < RG:
                        p = v * w[a]
                        acc[i][c] = p if acc[i][c] is None else acc[i][c] + p
    return acc


def filter_sums(pad, gpad, taps):
    rows, cols = gpad.shape[1] - 6, gpad.shape[2]
    for h in range(2):
        for first, count in ((0, 4), (4, 3)):

            def step(n, accs):
                r = first + n // 2
                base = (n % 2) * (cols // 2)
                for c in range(cols // 16):
                    xs = [pad[h, r, pl.ds(base + c * 8 + 5 + b, 8), :] for b in range(7)]
                    out = []
                    for k in range(count):
                        at = pl.ds(pl.multiple_of(base + c * 8, 8), 8)
                        g = gpad[h, r - (first + k) + 3, at, :]
                        out += [accs[k * 7 + b] + xs[b] * g for b in range(7)]
                    accs = tuple(out)
                return accs

            zero = jnp.zeros((8, LANES), F32)
            accs = lax.fori_loop(0, (rows + count - 1) * 2, step, (zero,) * (7 * count), unroll=8)
            for k in range(count):
                for b in range(7):
                    t = h * TAPS + (first + k) * 7 + b
                    taps[t : t + 1, :] = jnp.sum(accs[k * 7 + b], axis=0, keepdims=True)
        taps[h * TAPS + 49 : (h + 1) * TAPS, :] = jnp.zeros((TAPS - 49, LANES), F32)


def branch_kernel(
    tissue, upper, x_ref, top, bottom, left, right, cot, w_ref, bias, gain, shift, we, be, wr, scale,
    g_ref, g_left, g_right, g_top, g_bottom, kept, sent, taps, acc_ref, gpad, pad, wide, u_ref, nhat_ref, rstd_ref, normed, normed_t, go, go_t, hid, dz, dn,
):
    step = pl.program_id(0)
    rows, cols, chans = cot.shape
    hidden = we.shape[1]
    chunk = 256

    @pl.when(step == 0)
    def _():
        spread_weights(w_ref, wide, False)
        fill(pad, x_ref, top, bottom, left, right)
        acc_ref[...] = jnp.zeros_like(acc_ref)
        for h in range(2):
            for i in range(3):
                gpad[h, i] = jnp.zeros((cols, LANES), F32)
                gpad[h, x_ref.shape[0] + 3 + i] = jnp.zeros((cols, LANES), F32)

    ng = cols // (8 * CB)
    for h in range(2):

        def conv(n, _):
            row, col = (n // ng) * RG, (n % ng) * (8 * CB)
            acc = stencil(pad, wide, h, step * rows + row, col)
            for i in range(RG):
                for c in range(CB):
                    at = pl.multiple_of((row + i) * cols + col + c * 8, 8)
                    u_ref[pl.ds(at, 8), half(h)] = acc[i][c] + bias[0:1, half(h)]
            return 0

        lax.fori_loop(0, (rows // RG) * ng, conv, 0)

    tiles = cols // TILE
    for c in range(tiles):
        keep = tissue[step, c].astype(F32)
        part = cot[:, c * TILE : (c + 1) * TILE, :].astype(F32) * (scale[0:1, :] * keep)
        for i in range(rows):
            go[i * cols + c * TILE : i * cols + (c + 1) * TILE, :] = part[i].astype(BF16)

    def norm(i, _):
        at = pl.ds(pl.multiple_of(i * cols, cols), cols)
        u = u_ref[at, :]
        center = u - jnp.sum(u, axis=-1, keepdims=True) * (1.0 / chans)
        var = jnp.sum(center * center, axis=-1, keepdims=True) * (1.0 / chans)
        rstd = lax.rsqrt(var + 1e-06)
        nhat = center * rstd
        nhat_ref[at, :] = nhat
        rstd_ref[at, :] = jnp.broadcast_to(rstd, (cols, LANES))
        normed[at, :] = (nhat * gain[0:1, :] + shift[0:1, :]).astype(BF16)
        return 0

    lax.fori_loop(0, rows, norm, 0, unroll=4)
    normed_t[...] = normed[...].T
    go_t[...] = go[...].T

    for k in range(hidden // chunk):
        at = slice(k * chunk, (k + 1) * chunk)
        z = nn(normed[...], we[:, at]) + be[0:1, at]
        cdf = 0.5 * (1.0 + lax.erf(z * 0.7071067811865476))
        hid[:, at] = (z * cdf).astype(BF16)
        slope = cdf + z * jnp.exp(-0.5 * z * z) * 0.3989422804014327
        dz[:, at] = (nt(go[...], wr[at, :]) * slope).astype(BF16)
    dn[...] = nt(dz[...], we[...])
    acc_ref[0:chans, :] += nn(normed_t[...], dz[...])
    acc_ref[chans : 2 * chans, :] += nn(go_t[...], hid[...])

    def back(i, _):
        at = pl.ds(pl.multiple_of(i * cols, cols), cols)
        nhat = nhat_ref[at, :]
        d = dn[at, :] * gain[0:1, :]
        first = jnp.sum(d, axis=-1, keepdims=True) * (1.0 / chans)
        second = jnp.sum(d * nhat, axis=-1, keepdims=True) * (1.0 / chans)
        rstd = rstd_ref[at, :]
        g = (jnp.concatenate([rstd, rstd], axis=1) * (d - first - nhat * second)).astype(BF16)
        g_ref[step * rows + i] = g
        for h in range(2):
            gpad[h, step * rows + i + 3] = g[:, half(h)].astype(F32)
        return 0

    lax.fori_loop(0, rows, back, 0, unroll=4)

    @pl.when(step == pl.num_programs(0) - 1)
    def _():
        filter_sums(pad, gpad, taps)
        high = gpad.shape[1] - 6
        for h in range(2):
            for first, flat in ((3, g_top), (high, g_bottom)):
                for i in range(3):
                    flat[i * cols : (i + 1) * cols, half(h)] = gpad[h, first + i].astype(BF16)
            for col, flat in ((0, g_left), (cols - 3, g_right)):

                def collect(i, _, col=col, flat=flat, h=h):
                    v = [gpad[h, 3 + i * 16 + r, col : col + 3, :] for r in range(16)]
                    at = pl.ds(pl.multiple_of(i * 48, 16), 48)
                    flat[at, half(h)] = jnp.concatenate(v, axis=0).astype(BF16)
                    return 0

                lax.fori_loop(0, high // 16, collect, 0)
        blocks = hidden // LANES
        side = upper[0]
        for e in range(blocks):
            cut = half(e)
            other = acc_ref[chans : 2 * chans, cut].T
            count = 2 * TAPS // blocks
            piece = [acc_ref[0:chans, cut], other[:, :LANES], other[:, LANES:]]
            piece += [taps[e * count : (e + 1) * count, :], jnp.zeros((EXTRA - count, LANES), F32)]
            piece = jnp.concatenate(piece, axis=0)
            size = piece.shape[0]
            at = pl.ds((e % (blocks // 2)) * size, size)
            mine = side == e // (blocks // 2)

            @pl.when(mine)
            def _(piece=piece, at=at):
                kept[at, :] = piece

            @pl.when(jnp.logical_not(mine))
            def _(piece=piece, at=at):
                sent[at, :] = piece.astype(BF16)


def branch(x, halo, cot, tissue, upper, w, bias, gain, shift, we, be, wr, scale):
    rows, cols, chans = x.shape
    hidden = we.shape[1]
    pix = TILE * cols
    block = pl.BlockSpec((TILE, cols, chans), lambda s, t, u: (s, 0, 0))
    size = (2 * chans + EXTRA) * (hidden // LANES) // 2
    grid = pltpu.PrefetchScalarGridSpec(
        num_scalar_prefetch=2,
        grid=(rows // TILE,),
        in_specs=[VMEM] * 5 + [block] + [VMEM] * 8,
        out_specs=[VMEM] * 7,
        scratch_shapes=[
            pltpu.VMEM((2 * TAPS, LANES), F32),
            pltpu.VMEM((2 * chans, hidden), F32),
            pltpu.VMEM((2, rows + 6, cols, LANES), F32),
            pltpu.VMEM((2, rows + 6, cols + 16, LANES), F32),
            pltpu.VMEM((2, 49, 8, LANES), F32),
            pltpu.VMEM((pix, chans), F32),
            pltpu.VMEM((pix, chans), F32),
            pltpu.VMEM((pix, LANES), F32),
            pltpu.VMEM((pix, chans), BF16),
            pltpu.VMEM((chans, pix), BF16),
            pltpu.VMEM((pix, chans), BF16),
            pltpu.VMEM((chans, pix), BF16),
            pltpu.VMEM((pix, hidden), BF16),
            pltpu.VMEM((pix, hidden), BF16),
            pltpu.VMEM((pix, chans), F32),
        ],
    )
    return pl.pallas_call(
        branch_kernel,
        grid_spec=grid,
        out_shape=(
            jax.ShapeDtypeStruct(x.shape, BF16),
            jax.ShapeDtypeStruct((3 * rows, chans), BF16),
            jax.ShapeDtypeStruct((3 * rows, chans), BF16),
            jax.ShapeDtypeStruct((3 * cols, chans), BF16),
            jax.ShapeDtypeStruct((3 * cols, chans), BF16),
            jax.ShapeDtypeStruct((size, LANES), F32),
            jax.ShapeDtypeStruct((size, LANES), BF16),
        ),
        compiler_params=pltpu.CompilerParams(vmem_limit_bytes=40 << 20),
        cost_estimate=cost(42),
        name="branch",
    )(tissue, upper, x, *halo, cot, w, bias, gain, shift, we, be, wr, scale)


def cost(us):
    return pl.CostEstimate(flops=0, transcendentals=0, bytes_accessed=int(us * 3.69e6))


def input_kernel(part, g_ref, top, bottom, left, right, cot, w_ref, *rest):
    o_ref, pad, wide, out = rest[-4:]
    rows, cols, _ = out.shape
    base = part * rows
    spread_weights(w_ref, wide, True)
    fill(pad, g_ref, top, bottom, left, right, base, rows)
    ng = cols // (8 * CB)
    for h in range(2):

        def conv(n, _):
            row, col = (n // ng) * RG, (n % ng) * (8 * CB)
            acc = stencil(pad, wide, h, row, col)
            for i in range(RG):
                for c in range(CB):
                    at = pl.ds(pl.multiple_of(col + c * 8, 8), 8)
                    out[row + i, at, half(h)] = acc[i][c]
            return 0

        lax.fori_loop(0, (rows // RG) * ng, conv, 0)

    def last(i, _):
        o_ref[i] = (cot[base + i].astype(F32) + out[i]).astype(BF16)
        return 0

    lax.fori_loop(0, rows, last, 0, unroll=4)


def input_grad(g, halo, cot, w, so_far, part):
    _, cols, chans = g.shape
    arrays = (g, *halo, cot, w)
    specs = [VMEM] * len(arrays)
    alias = {}
    if so_far is not None:
        alias = {len(arrays): 0}
        arrays += (so_far,)
        specs.append(pl.BlockSpec(memory_space=pl.ANY))
    return pl.pallas_call(
        functools.partial(input_kernel, part),
        grid=(1,),
        out_shape=jax.ShapeDtypeStruct(g.shape, BF16),
        in_specs=specs,
        out_specs=pl.BlockSpec((PART, cols, chans), lambda s: (part, 0, 0)),
        scratch_shapes=[
            pltpu.VMEM((2, PART + 6, cols + 16, LANES), F32),
            pltpu.VMEM((2, 49, 8, LANES), F32),
            pltpu.VMEM((PART, cols, chans), F32),
        ],
        input_output_aliases=alias,
        compiler_params=pltpu.CompilerParams(vmem_limit_bytes=16 << 20),
        cost_estimate=cost(4),
        name="input_grad",
    )(*arrays)


def spread_kernel(upper, mine, other, taps_ref, expand, reduce, *, factor):
    chans = expand.shape[0]
    blocks = expand.shape[1] // LANES
    size = 2 * chans + EXTRA
    count = 2 * TAPS // blocks
    for e in range(blocks):
        at = pl.ds((e % (blocks // 2)) * size, size)
        here = upper[0] == e // (blocks // 2)

        def write(flat, e=e, at=at):
            v = flat[at, :].astype(F32) * factor
            expand[:, half(e)] = v[:chans]
            for h in range(2):
                reduce[half(e), half(h)] = v[chans + h * LANES : chans + (h + 1) * LANES]
            h, first = e * count // TAPS, e * count % TAPS
            taps_ref[first : first + count, half(h)] = v[2 * chans : 2 * chans + count]

        pl.when(here)(functools.partial(write, mine))
        pl.when(jnp.logical_not(here))(functools.partial(write, other))


def spread(upper, mine, other, chans, hidden, factor):
    grid = pltpu.PrefetchScalarGridSpec(
        num_scalar_prefetch=1,
        grid=(1,),
        in_specs=[VMEM] * 2,
        out_specs=[
            pl.BlockSpec(shape, lambda s, u: (0, 0))
            for shape in ((TAPS, chans), (chans, hidden), (hidden, chans))
        ],
    )
    return pl.pallas_call(
        functools.partial(spread_kernel, factor=factor),
        grid_spec=grid,
        out_shape=(
            jax.ShapeDtypeStruct((TAPS, chans), F32),
            jax.ShapeDtypeStruct((chans, hidden), F32),
            jax.ShapeDtypeStruct((hidden, chans), F32),
        ),
        compiler_params=pltpu.CompilerParams(vmem_limit_bytes=12 << 20),
        cost_estimate=cost(2),
        name="spread",
    )(upper, mine, other)


AXES = ("y", "x_hi", "core", "z", "x_lo")
SIZES = (4, 2, 2, 8, 2)
TY, TX = AXES[:3], AXES[3:]


def beside(value, axes, odd):
    count = math.prod(SIZES[AXES.index(a)] for a in axes)
    pairs = [(i, i + 1) for i in range(odd, count - 1, 2)]
    return lax.ppermute(value, axes, pairs + [(b, a) for a, b in pairs])


def both_sides(low, high, axes):
    odd = lax.axis_index(axes) % 2 == 1
    first = beside(jnp.where(odd, low, high), axes, 0)
    second = beside(jnp.where(odd, high, low), axes, 1)
    return jnp.where(odd, first, second), jnp.where(odd, second, first)


def halo_of(left, right, top, bottom):
    chans = left.shape[1]
    left, right = both_sides(left, right, TX)
    filler = jnp.zeros((14, chans), BF16)
    top = jnp.concatenate([top, left[:9], right[:9], filler])
    bottom = jnp.concatenate([bottom, left[-9:], right[-9:], filler])
    top, bottom = both_sides(top, bottom, TY)
    return top, bottom, left, right


SWAPS = {
    "core": (("core",), ("core",)),
    "x_near": (("x_lo",), ("x_lo", "x_hi")),
    "x_far": (("x_lo", "x_hi"), ("x_hi",)),
    "y_near": ((("y", 1),), (("y", 1), ("y", 2))),
    "y_far": ((("y", 3),), (("y", 2),)),
}


def keeps_upper(name):
    bit = 0
    for item in SWAPS[name][1]:
        axis, mask = item if isinstance(item, tuple) else (item, 1)
        bit = bit + (lax.axis_index(axis) // mask) % 2
    return bit % 2


def swap(value, name):
    index = np.arange(math.prod(SIZES)).reshape(SIZES)
    where = np.indices(SIZES)
    for item in SWAPS[name][0]:
        axis, mask = item if isinstance(item, tuple) else (item, 1)
        where[AXES.index(axis)] ^= mask
    other = index[tuple(where)]
    pairs = [(int(a), int(b)) for a, b in zip(index.ravel(), other.ravel())]
    return lax.ppermute(value, AXES, pairs)


def total(kept, sent):
    names = list(SWAPS)
    for n, name in enumerate(names):
        kept = kept + swap(sent, name).astype(F32)
        if n + 1 < len(names):
            upper = keeps_upper(names[n + 1]) == 1
            size = kept.shape[0] // 2
            low, high = kept[:size], kept[size:]
            sent = jnp.where(upper, low, high).astype(BF16)
            kept = jnp.where(upper, high, low)
    count = SIZES[AXES.index("z")]
    copies = jnp.broadcast_to(kept.astype(BF16)[None], (count, *kept.shape))
    copies = lax.all_to_all(copies, "z", 0, 0, tiled=True)
    out = jnp.sum(copies.astype(F32), axis=0).astype(BF16)
    for name in reversed(names):
        upper = keeps_upper(name) == 1
        other = swap(out, name)
        if name == "core":
            return out, other
        out = jnp.concatenate([jnp.where(upper, other, out), jnp.where(upper, out, other)])


def body(x, cot, tissue, w, bias, gain, shift, we, be, wr, scale):
    rows, cols, chans = x.shape
    line = lambda v: v.reshape(1, -1)
    sizes = (math.prod(SIZES[:3]), math.prod(SIZES[3:]))
    factor = 1.0 / math.sqrt(rows * sizes[0] * cols * sizes[1])
    edges = (x[:, :3], x[:, cols - 3 :], x[:3], x[rows - 3 :])
    halo = halo_of(*(v.reshape(-1, chans) for v in edges))
    upper = keeps_upper("core").astype(jnp.int32).reshape(1)
    rest = (w, line(bias), line(gain), line(shift), we, line(be), wr, line(scale))
    g, *edges, kept, sent = branch(x, halo, cot, tissue, upper, *rest)
    ghalo = halo_of(*edges)
    result = None
    for part in range(rows // PART):
        result = input_grad(g, ghalo, cot, w, result, part)
    mine, other = total(kept, sent)
    taps, expand, reduce = spread(upper, mine, other, chans, we.shape[1], factor)
    return result, taps[: w.shape[0]], expand, reduce


def solution(mesh):
    fine = Mesh(mesh.devices.reshape(SIZES), AXES)
    pixels = P(TY, TX, None)
    return jax.shard_map(
        body,
        mesh=fine,
        in_specs=(pixels, pixels, P(TY, TX)) + (P(),) * 8,
        out_specs=(pixels, P(), P(), P()),
        check_vma=False,
    )
```

```python
import functools
import math

import jax
import jax.numpy as jnp
import numpy as np
from jax import lax
from jax.experimental import pallas as pl
from jax.experimental.pallas import tpu as pltpu
from jax.sharding import Mesh, PartitionSpec as P


F32, BF16 = jnp.float32, jnp.bfloat16
TILE = 16
LANES = 128
RG = 8
CB = 3
TAPS = 64
PART = 16
EXTRA = 32
VMEM = pl.BlockSpec(memory_space=pltpu.VMEM)


def nn(a, b):
    return lax.dot_general(a, b, (((1,), (0,)), ((), ())), preferred_element_type=F32)


def nt(a, b):
    return lax.dot_general(a, b, (((1,), (1,)), ((), ())), preferred_element_type=F32)


def half(h):
    return slice(h * LANES, (h + 1) * LANES)


def spread_weights(w_ref, wide, flip, halves=(0, 1)):
    for k, h in enumerate(halves):
        for t in range(49):
            s = 48 - t if flip else t
            wide[k, t] = jnp.broadcast_to(w_ref[s : s + 1, half(h)], (8, LANES))


def fill(pad, core, top, bottom, left, right, base=0, count=None):
    rows, cols = core.shape[0], core.shape[1]
    count = rows if count is None else count
    ends = (5, 8 + cols)
    first, stop = max(base - 3, 0), min(base + count + 3, rows)
    edges = []
    if base == 0:
        edges.append((0, top))
    if base + count == rows:
        edges.append((3 + count, bottom))
    for h in range(2):

        def put(i, _):
            pad[h, i - base + 3, 8 : 8 + cols, :] = core[i, :, half(h)].astype(F32)
            return 0

        lax.fori_loop(first, stop, put, 0, unroll=4 if (stop - first) % 4 == 0 else 1)
        for at, flat in edges:
            extra = flat[3 * cols : 3 * cols + 24, half(h)].astype(F32)
            for i in range(3):
                line = flat[i * cols : (i + 1) * cols, half(h)].astype(F32)
                pad[h, at + i, 8 : 8 + cols, :] = line
                for n, end in enumerate(ends):
                    corner = extra[n * 9 + i * 3 : n * 9 + i * 3 + 3]
                    pad[h, at + i, end : end + 3, :] = corner

        def side(start, lines):
            at = pl.ds(pl.multiple_of(start * 3, 8), 24)
            for end, flat in zip(ends, (left, right)):
                v = flat[at, half(h)].astype(F32)
                for r in lines:
                    pad[h, 3 - base + start + r, end : end + 3, :] = v[r * 3 : r * 3 + 3]

        def eight(i, _):
            side(base + i * 8, range(8))
            return 0

        lax.fori_loop(0, count // 8, eight, 0)
        if first < base:
            side(base - 8, range(8 - (base - first), 8))
        if stop > base + count:
            side(base + count, range(stop - base - count))


def stencil(pad, wide, h, row, col):
    acc = [[None] * CB for _ in range(RG)]
    for b in range(7):
        w = [wide[h, a * 7 + b] for a in range(7)]
        for r in range(RG + 6):
            for c in range(CB):
                v = pad[h, row + r, pl.ds(col + c * 8 + 5 + b, 8), :]
                for a in range(7):
                    i = r - a
                    if 0 <= i < RG:
                        p = v * w[a]
                        acc[i][c] = p if acc[i][c] is None else acc[i][c] + p
    return acc


def filter_sums(pad, gpad, taps):
    rows, cols = gpad.shape[1] - 6, gpad.shape[2]
    for h in range(2):
        for first, count in ((0, 4), (4, 3)):

            def step(n, accs):
                r = first + n // 2
                base = (n % 2) * (cols // 2)
                for c in range(cols // 16):
                    xs = [pad[h, r, pl.ds(base + c * 8 + 5 + b, 8), :] for b in range(7)]
                    out = []
                    for k in range(count):
                        at = pl.ds(pl.multiple_of(base + c * 8, 8), 8)
                        g = gpad[h, r - (first + k) + 3, at, :]
                        out += [accs[k * 7 + b] + xs[b] * g for b in range(7)]
                    accs = tuple(out)
                return accs

            zero = jnp.zeros((8, LANES), F32)
            accs = lax.fori_loop(0, (rows + count - 1) * 2, step, (zero,) * (7 * count), unroll=8)
            for k in range(count):
                for b in range(7):
                    t = h * TAPS + (first + k) * 7 + b
                    taps[t : t + 1, :] = jnp.sum(accs[k * 7 + b], axis=0, keepdims=True)
        taps[h * TAPS + 49 : (h + 1) * TAPS, :] = jnp.zeros((TAPS - 49, LANES), F32)


def branch_kernel(
    tissue, upper, x_ref, top, bottom, left, right, cot, w_ref, bias, gain, shift, we, be, wr, scale,
    g_ref, g_left, g_right, g_top, g_bottom, kept, sent, taps, acc_ref, gpad, pad, wide, u_ref, nhat_ref, rstd_ref, normed, normed_t, go, go_t, hid, dz, dn,
):
    step = pl.program_id(0)
    rows, cols, chans = cot.shape
    hidden = we.shape[1]
    chunk = 256

    @pl.when(step == 0)
    def _():
        spread_weights(w_ref, wide, False)
        fill(pad, x_ref, top, bottom, left, right)
        acc_ref[...] = jnp.zeros_like(acc_ref)
        for h in range(2):
            for i in range(3):
                gpad[h, i] = jnp.zeros((cols, LANES), F32)
                gpad[h, x_ref.shape[0] + 3 + i] = jnp.zeros((cols, LANES), F32)

    ng = cols // (8 * CB)
    for h in range(2):

        def conv(n, _):
            row, col = (n // ng) * RG, (n % ng) * (8 * CB)
            acc = stencil(pad, wide, h, step * rows + row, col)
            for i in range(RG):
                for c in range(CB):
                    at = pl.multiple_of((row + i) * cols + col + c * 8, 8)
                    u_ref[pl.ds(at, 8), half(h)] = acc[i][c] + bias[0:1, half(h)]
            return 0

        lax.fori_loop(0, (rows // RG) * ng, conv, 0)

    tiles = cols // TILE
    for c in range(tiles):
        keep = tissue[step, c].astype(F32)
        part = cot[:, c * TILE : (c + 1) * TILE, :].astype(F32) * (scale[0:1, :] * keep)
        for i in range(rows):
            go[i * cols + c * TILE : i * cols + (c + 1) * TILE, :] = part[i].astype(BF16)

    def norm(i, _):
        at = pl.ds(pl.multiple_of(i * cols, cols), cols)
        u = u_ref[at, :]
        center = u - jnp.sum(u, axis=-1, keepdims=True) * (1.0 / chans)
        var = jnp.sum(center * center, axis=-1, keepdims=True) * (1.0 / chans)
        rstd = lax.rsqrt(var + 1e-06)
        nhat = center * rstd
        nhat_ref[at, :] = nhat
        rstd_ref[at, :] = jnp.broadcast_to(rstd, (cols, LANES))
        normed[at, :] = (nhat * gain[0:1, :] + shift[0:1, :]).astype(BF16)
        return 0

    lax.fori_loop(0, rows, norm, 0, unroll=4)
    normed_t[...] = normed[...].T
    go_t[...] = go[...].T

    for k in range(hidden // chunk):
        at = slice(k * chunk, (k + 1) * chunk)
        z = nn(normed[...], we[:, at]) + be[0:1, at]
        cdf = 0.5 * (1.0 + lax.erf(z * 0.7071067811865476))
        hid[:, at] = (z * cdf).astype(BF16)
        slope = cdf + z * jnp.exp(-0.5 * z * z) * 0.3989422804014327
        dz[:, at] = (nt(go[...], wr[at, :]) * slope).astype(BF16)
    dn[...] = nt(dz[...], we[...])
    acc_ref[0:chans, :] += nn(normed_t[...], dz[...])
    acc_ref[chans : 2 * chans, :] += nn(go_t[...], hid[...])

    def back(i, _):
        at = pl.ds(pl.multiple_of(i * cols, cols), cols)
        nhat = nhat_ref[at, :]
        d = dn[at, :] * gain[0:1, :]
        first = jnp.sum(d, axis=-1, keepdims=True) * (1.0 / chans)
        second = jnp.sum(d * nhat, axis=-1, keepdims=True) * (1.0 / chans)
        rstd = rstd_ref[at, :]
        g = (jnp.concatenate([rstd, rstd], axis=1) * (d - first - nhat * second)).astype(BF16)
        g_ref[step * rows + i] = g
        for h in range(2):
            gpad[h, step * rows + i + 3] = g[:, half(h)].astype(F32)
        return 0

    lax.fori_loop(0, rows, back, 0, unroll=4)

    @pl.when(step == pl.num_programs(0) - 1)
    def _():
        filter_sums(pad, gpad, taps)
        high = gpad.shape[1] - 6
        for h in range(2):
            for first, flat in ((3, g_top), (high, g_bottom)):
                for i in range(3):
                    flat[i * cols : (i + 1) * cols, half(h)] = gpad[h, first + i].astype(BF16)
            for col, flat in ((0, g_left), (cols - 3, g_right)):

                def collect(i, _, col=col, flat=flat, h=h):
                    v = [gpad[h, 3 + i * 16 + r, col : col + 3, :] for r in range(16)]
                    at = pl.ds(pl.multiple_of(i * 48, 16), 48)
                    flat[at, half(h)] = jnp.concatenate(v, axis=0).astype(BF16)
                    return 0

                lax.fori_loop(0, high // 16, collect, 0)
        blocks = hidden // LANES
        side = upper[0]
        for e in range(blocks):
            cut = half(e)
            other = acc_ref[chans : 2 * chans, cut].T
            count = 2 * TAPS // blocks
            piece = [acc_ref[0:chans, cut], other[:, :LANES], other[:, LANES:]]
            piece += [taps[e * count : (e + 1) * count, :], jnp.zeros((EXTRA - count, LANES), F32)]
            piece = jnp.concatenate(piece, axis=0)
            size = piece.shape[0]
            at = pl.ds((e % (blocks // 2)) * size, size)
            mine = side == e // (blocks // 2)

            @pl.when(mine)
            def _(piece=piece, at=at):
                kept[at, :] = piece

            @pl.when(jnp.logical_not(mine))
            def _(piece=piece, at=at):
                sent[at, :] = piece.astype(BF16)


def branch(x, halo, cot, tissue, upper, w, bias, gain, shift, we, be, wr, scale):
    rows, cols, chans = x.shape
    hidden = we.shape[1]
    pix = TILE * cols
    block = pl.BlockSpec((TILE, cols, chans), lambda s, t, u: (s, 0, 0))
    whole = lambda *shape: pl.BlockSpec(shape, lambda s, t, u: (0, 0))
    size = (2 * chans + EXTRA) * (hidden // LANES) // 2
    grid = pltpu.PrefetchScalarGridSpec(
        num_scalar_prefetch=2,
        grid=(rows // TILE,),
        in_specs=[VMEM] * 5 + [block] + [VMEM] * 8,
        out_specs=[pl.BlockSpec((rows, cols, chans), lambda s, t, u: (0, 0, 0))]
        + [whole(3 * rows, chans)] * 2
        + [whole(3 * cols, chans)] * 2
        + [whole(size, LANES)] * 2,
        scratch_shapes=[
            pltpu.VMEM((2 * TAPS, LANES), F32),
            pltpu.VMEM((2 * chans, hidden), F32),
            pltpu.VMEM((2, rows + 6, cols, LANES), F32),
            pltpu.VMEM((2, rows + 6, cols + 16, LANES), F32),
            pltpu.VMEM((2, 49, 8, LANES), F32),
            pltpu.VMEM((pix, chans), F32),
            pltpu.VMEM((pix, chans), F32),
            pltpu.VMEM((pix, LANES), F32),
            pltpu.VMEM((pix, chans), BF16),
            pltpu.VMEM((chans, pix), BF16),
            pltpu.VMEM((pix, chans), BF16),
            pltpu.VMEM((chans, pix), BF16),
            pltpu.VMEM((pix, hidden), BF16),
            pltpu.VMEM((pix, hidden), BF16),
            pltpu.VMEM((pix, chans), F32),
        ],
    )
    return pl.pallas_call(
        branch_kernel,
        grid_spec=grid,
        out_shape=(
            jax.ShapeDtypeStruct(x.shape, BF16),
            jax.ShapeDtypeStruct((3 * rows, chans), BF16),
            jax.ShapeDtypeStruct((3 * rows, chans), BF16),
            jax.ShapeDtypeStruct((3 * cols, chans), BF16),
            jax.ShapeDtypeStruct((3 * cols, chans), BF16),
            jax.ShapeDtypeStruct((size, LANES), F32),
            jax.ShapeDtypeStruct((size, LANES), BF16),
        ),
        compiler_params=pltpu.CompilerParams(vmem_limit_bytes=56 << 20),
        cost_estimate=cost(42),
        name="branch",
    )(tissue, upper, x, *halo, cot, w, bias, gain, shift, we, be, wr, scale)


def cost(us):
    return pl.CostEstimate(flops=0, transcendentals=0, bytes_accessed=int(us * 3.69e6))


def input_kernel(part, g_ref, top, bottom, left, right, cot, w_ref, *rest):
    o_ref, pad, wide, out = rest[-4:]
    rows, cols, _ = out.shape
    base = part * rows
    spread_weights(w_ref, wide, True)
    fill(pad, g_ref, top, bottom, left, right, base, rows)
    ng = cols // (8 * CB)
    for h in range(2):

        def conv(n, _):
            row, col = (n // ng) * RG, (n % ng) * (8 * CB)
            acc = stencil(pad, wide, h, row, col)
            for i in range(RG):
                for c in range(CB):
                    at = pl.ds(pl.multiple_of(col + c * 8, 8), 8)
                    out[row + i, at, half(h)] = acc[i][c]
            return 0

        lax.fori_loop(0, (rows // RG) * ng, conv, 0)

    def last(i, _):
        o_ref[i] = (cot[base + i].astype(F32) + out[i]).astype(BF16)
        return 0

    lax.fori_loop(0, rows, last, 0, unroll=4)


def input_grad(g, halo, cot, w, so_far, part):
    _, cols, chans = g.shape
    arrays = (g, *halo, cot, w)
    specs = [VMEM] * len(arrays)
    alias = {}
    if so_far is not None:
        alias = {len(arrays): 0}
        arrays += (so_far,)
        specs.append(pl.BlockSpec(memory_space=pl.ANY))
    return pl.pallas_call(
        functools.partial(input_kernel, part),
        grid=(1,),
        out_shape=jax.ShapeDtypeStruct(g.shape, BF16),
        in_specs=specs,
        out_specs=pl.BlockSpec((PART, cols, chans), lambda s: (part, 0, 0)),
        scratch_shapes=[
            pltpu.VMEM((2, PART + 6, cols + 16, LANES), F32),
            pltpu.VMEM((2, 49, 8, LANES), F32),
            pltpu.VMEM((PART, cols, chans), F32),
        ],
        input_output_aliases=alias,
        compiler_params=pltpu.CompilerParams(vmem_limit_bytes=16 << 20),
        cost_estimate=cost(4),
        name="input_grad",
    )(*arrays)


def spread_kernel(upper, mine, other, taps_ref, expand, reduce, *, factor):
    chans = expand.shape[0]
    blocks = expand.shape[1] // LANES
    size = 2 * chans + EXTRA
    count = 2 * TAPS // blocks
    for e in range(blocks):
        at = pl.ds((e % (blocks // 2)) * size, size)
        here = upper[0] == e // (blocks // 2)

        def write(flat, e=e, at=at):
            v = flat[at, :].astype(F32) * factor
            expand[:, half(e)] = v[:chans]
            for h in range(2):
                reduce[half(e), half(h)] = v[chans + h * LANES : chans + (h + 1) * LANES]
            h, first = e * count // TAPS, e * count % TAPS
            taps_ref[first : first + count, half(h)] = v[2 * chans : 2 * chans + count]

        pl.when(here)(functools.partial(write, mine))
        pl.when(jnp.logical_not(here))(functools.partial(write, other))


def spread(upper, mine, other, chans, hidden, factor):
    grid = pltpu.PrefetchScalarGridSpec(
        num_scalar_prefetch=1,
        grid=(1,),
        in_specs=[VMEM] * 2,
        out_specs=[
            pl.BlockSpec(shape, lambda s, u: (0, 0))
            for shape in ((TAPS, chans), (chans, hidden), (hidden, chans))
        ],
    )
    return pl.pallas_call(
        functools.partial(spread_kernel, factor=factor),
        grid_spec=grid,
        out_shape=(
            jax.ShapeDtypeStruct((TAPS, chans), F32),
            jax.ShapeDtypeStruct((chans, hidden), F32),
            jax.ShapeDtypeStruct((hidden, chans), F32),
        ),
        compiler_params=pltpu.CompilerParams(vmem_limit_bytes=12 << 20),
        cost_estimate=cost(2),
        name="spread",
    )(upper, mine, other)


AXES = ("y", "x_hi", "core", "z", "x_lo")
SIZES = (4, 2, 2, 8, 2)
TY, TX = AXES[:3], AXES[3:]


def beside(value, axes, odd):
    count = math.prod(SIZES[AXES.index(a)] for a in axes)
    pairs = [(i, i + 1) for i in range(odd, count - 1, 2)]
    return lax.ppermute(value, axes, pairs + [(b, a) for a, b in pairs])


def both_sides(low, high, axes):
    odd = lax.axis_index(axes) % 2 == 1
    first = beside(jnp.where(odd, low, high), axes, 0)
    second = beside(jnp.where(odd, high, low), axes, 1)
    return jnp.where(odd, first, second), jnp.where(odd, second, first)


def halo_of(left, right, top, bottom):
    chans = left.shape[1]
    left, right = both_sides(left, right, TX)
    filler = jnp.zeros((14, chans), BF16)
    top = jnp.concatenate([top, left[:9], right[:9], filler])
    bottom = jnp.concatenate([bottom, left[-9:], right[-9:], filler])
    top, bottom = both_sides(top, bottom, TY)
    return top, bottom, left, right


SWAPS = {
    "core": (("core",), ("core",)),
    "x_near": (("x_lo",), ("x_lo", "x_hi")),
    "x_far": (("x_lo", "x_hi"), ("x_hi",)),
    "y_near": ((("y", 1),), (("y", 1), ("y", 2))),
    "y_far": ((("y", 3),), (("y", 2),)),
}


def keeps_upper(name):
    bit = 0
    for item in SWAPS[name][1]:
        axis, mask = item if isinstance(item, tuple) else (item, 1)
        bit = bit + (lax.axis_index(axis) // mask) % 2
    return bit % 2


def swap(value, name):
    index = np.arange(math.prod(SIZES)).reshape(SIZES)
    where = np.indices(SIZES)
    for item in SWAPS[name][0]:
        axis, mask = item if isinstance(item, tuple) else (item, 1)
        where[AXES.index(axis)] ^= mask
    other = index[tuple(where)]
    pairs = [(int(a), int(b)) for a, b in zip(index.ravel(), other.ravel())]
    return lax.ppermute(value, AXES, pairs)


def total(kept, sent):
    names = list(SWAPS)
    for n, name in enumerate(names):
        kept = kept + swap(sent, name).astype(F32)
        if n + 1 < len(names):
            upper = keeps_upper(names[n + 1]) == 1
            size = kept.shape[0] // 2
            low, high = kept[:size], kept[size:]
            sent = jnp.where(upper, low, high).astype(BF16)
            kept = jnp.where(upper, high, low)
    count = SIZES[AXES.index("z")]
    copies = jnp.broadcast_to(kept.astype(BF16)[None], (count, *kept.shape))
    copies = lax.all_to_all(copies, "z", 0, 0, tiled=True)
    out = jnp.sum(copies.astype(F32), axis=0).astype(BF16)
    for name in reversed(names):
        upper = keeps_upper(name) == 1
        other = swap(out, name)
        if name == "core":
            return out, other
        out = jnp.concatenate([jnp.where(upper, other, out), jnp.where(upper, out, other)])


def body(x, cot, tissue, w, bias, gain, shift, we, be, wr, scale):
    rows, cols, chans = x.shape
    line = lambda v: v.reshape(1, -1)
    sizes = (math.prod(SIZES[:3]), math.prod(SIZES[3:]))
    factor = 1.0 / math.sqrt(rows * sizes[0] * cols * sizes[1])
    edges = (x[:, :3], x[:, cols - 3 :], x[:3], x[rows - 3 :])
    halo = halo_of(*(v.reshape(-1, chans) for v in edges))
    upper = keeps_upper("core").astype(jnp.int32).reshape(1)
    rest = (w, line(bias), line(gain), line(shift), we, line(be), wr, line(scale))
    g, *edges, kept, sent = branch(x, halo, cot, tissue, upper, *rest)
    ghalo = halo_of(*edges)
    result = None
    for part in range(rows // PART):
        result = input_grad(g, ghalo, cot, w, result, part)
    mine, other = total(kept, sent)
    taps, expand, reduce = spread(upper, mine, other, chans, we.shape[1], factor)
    return result, taps[: w.shape[0]], expand, reduce


def solution(mesh):
    fine = Mesh(mesh.devices.reshape(SIZES), AXES)
    pixels = P(TY, TX, None)
    return jax.shard_map(
        body,
        mesh=fine,
        in_specs=(pixels, pixels, P(TY, TX)) + (P(),) * 8,
        out_specs=(pixels, P(), P(), P()),
        check_vma=False,
    )
```

```python
import functools
import math

import jax
import jax.numpy as jnp
import numpy as np
from jax import lax
from jax.experimental import pallas as pl
from jax.experimental.pallas import tpu as pltpu
from jax.sharding import Mesh, PartitionSpec as P


F32, BF16 = jnp.float32, jnp.bfloat16
TILE = 16
LANES = 128
RG = 8
CB = 3
TAPS = 64
PART = 16
EXTRA = 32
VMEM = pl.BlockSpec(memory_space=pltpu.VMEM)


def nn(a, b):
    return lax.dot_general(a, b, (((1,), (0,)), ((), ())), preferred_element_type=F32)


def nt(a, b):
    return lax.dot_general(a, b, (((1,), (1,)), ((), ())), preferred_element_type=F32)


def half(h):
    return slice(h * LANES, (h + 1) * LANES)


def spread_weights(w_ref, wide, flip, halves=(0, 1)):
    for k, h in enumerate(halves):
        for t in range(49):
            s = 48 - t if flip else t
            wide[k, t] = jnp.broadcast_to(w_ref[s : s + 1, half(h)], (8, LANES))


def fill(pad, core, top, bottom, left, right, base=0, count=None):
    rows, cols = core.shape[0], core.shape[1]
    count = rows if count is None else count
    ends = (5, 8 + cols)
    first, stop = max(base - 3, 0), min(base + count + 3, rows)
    edges = []
    if base == 0:
        edges.append((0, top))
    if base + count == rows:
        edges.append((3 + count, bottom))
    for h in range(2):

        def put(i, _):
            pad[h, i - base + 3, 8 : 8 + cols, :] = core[i, :, half(h)].astype(F32)
            return 0

        lax.fori_loop(first, stop, put, 0, unroll=4 if (stop - first) % 4 == 0 else 1)
        for at, flat in edges:
            extra = flat[3 * cols : 3 * cols + 24, half(h)].astype(F32)
            for i in range(3):
                line = flat[i * cols : (i + 1) * cols, half(h)].astype(F32)
                pad[h, at + i, 8 : 8 + cols, :] = line
                for n, end in enumerate(ends):
                    corner = extra[n * 9 + i * 3 : n * 9 + i * 3 + 3]
                    pad[h, at + i, end : end + 3, :] = corner

        def side(start, lines):
            at = pl.ds(pl.multiple_of(start * 3, 8), 24)
            for end, flat in zip(ends, (left, right)):
                v = flat[at, half(h)].astype(F32)
                for r in lines:
                    pad[h, 3 - base + start + r, end : end + 3, :] = v[r * 3 : r * 3 + 3]

        def eight(i, _):
            side(base + i * 8, range(8))
            return 0

        lax.fori_loop(0, count // 8, eight, 0)
        if first < base:
            side(base - 8, range(8 - (base - first), 8))
        if stop > base + count:
            side(base + count, range(stop - base - count))


def stencil(pad, wide, h, row, col):
    acc = [[None] * CB for _ in range(RG)]
    for b in range(7):
        w = [wide[h, a * 7 + b] for a in range(7)]
        for r in range(RG + 6):
            for c in range(CB):
                v = pad[h, row + r, pl.ds(col + c * 8 + 5 + b, 8), :]
                for a in range(7):
                    i = r - a
                    if 0 <= i < RG:
                        p = v * w[a]
                        acc[i][c] = p if acc[i][c] is None else acc[i][c] + p
    return acc


def filter_sums(pad, gpad, taps):
    rows, cols = gpad.shape[1] - 6, gpad.shape[2]
    for h in range(2):
        for first, count in ((0, 4), (4, 3)):

            def step(n, accs):
                r = first + n // 2
                base = (n % 2) * (cols // 2)
                for c in range(cols // 16):
                    xs = [pad[h, r, pl.ds(base + c * 8 + 5 + b, 8), :] for b in range(7)]
                    out = []
                    for k in range(count):
                        at = pl.ds(pl.multiple_of(base + c * 8, 8), 8)
                        g = gpad[h, r - (first + k) + 3, at, :]
                        out += [accs[k * 7 + b] + xs[b] * g for b in range(7)]
                    accs = tuple(out)
                return accs

            zero = jnp.zeros((8, LANES), F32)
            accs = lax.fori_loop(0, (rows + count - 1) * 2, step, (zero,) * (7 * count), unroll=8)
            for k in range(count):
                for b in range(7):
                    t = h * TAPS + (first + k) * 7 + b
                    taps[t : t + 1, :] = jnp.sum(accs[k * 7 + b], axis=0, keepdims=True)
        taps[h * TAPS + 49 : (h + 1) * TAPS, :] = jnp.zeros((TAPS - 49, LANES), F32)


def branch_kernel(
    tissue, upper, x_ref, top, bottom, left, right, cot, w_ref, bias, gain, shift, we, be, wr, scale,
    g_ref, g_left, g_right, g_top, g_bottom, kept, sent, taps, acc_ref, gpad, pad, wide, u_ref, nhat_ref, rstd_ref, normed, normed_t, go, go_t, hid, dz, dn,
):
    step = pl.program_id(0)
    rows, cols, chans = cot.shape
    hidden = we.shape[1]
    chunk = 256

    @pl.when(step == 0)
    def _():
        spread_weights(w_ref, wide, False)
        fill(pad, x_ref, top, bottom, left, right)
        acc_ref[...] = jnp.zeros_like(acc_ref)
        for h in range(2):
            for i in range(3):
                gpad[h, i] = jnp.zeros((cols, LANES), F32)
                gpad[h, x_ref.shape[0] + 3 + i] = jnp.zeros((cols, LANES), F32)

    ng = cols // (8 * CB)
    for h in range(2):

        def conv(n, _):
            row, col = (n // ng) * RG, (n % ng) * (8 * CB)
            acc = stencil(pad, wide, h, step * rows + row, col)
            for i in range(RG):
                for c in range(CB):
                    at = pl.multiple_of((row + i) * cols + col + c * 8, 8)
                    u_ref[pl.ds(at, 8), half(h)] = acc[i][c] + bias[0:1, half(h)]
            return 0

        lax.fori_loop(0, (rows // RG) * ng, conv, 0)

    tiles = cols // TILE
    for c in range(tiles):
        keep = tissue[step, c].astype(F32)
        part = cot[:, c * TILE : (c + 1) * TILE, :].astype(F32) * (scale[0:1, :] * keep)
        for i in range(rows):
            go[i * cols + c * TILE : i * cols + (c + 1) * TILE, :] = part[i].astype(BF16)

    def norm(i, _):
        at = pl.ds(pl.multiple_of(i * cols, cols), cols)
        u = u_ref[at, :]
        center = u - jnp.sum(u, axis=-1, keepdims=True) * (1.0 / chans)
        var = jnp.sum(center * center, axis=-1, keepdims=True) * (1.0 / chans)
        rstd = lax.rsqrt(var + 1e-06)
        nhat = center * rstd
        nhat_ref[at, :] = nhat
        rstd_ref[at, :] = jnp.broadcast_to(rstd, (cols, LANES))
        normed[at, :] = (nhat * gain[0:1, :] + shift[0:1, :]).astype(BF16)
        return 0

    lax.fori_loop(0, rows, norm, 0, unroll=4)
    normed_t[...] = normed[...].T
    go_t[...] = go[...].T

    for k in range(hidden // chunk):
        at = slice(k * chunk, (k + 1) * chunk)
        z = nn(normed[...], we[:, at]) + be[0:1, at]
        cdf = 0.5 * (1.0 + lax.erf(z * 0.7071067811865476))
        hid[:, at] = (z * cdf).astype(BF16)
        slope = cdf + z * jnp.exp(-0.5 * z * z) * 0.3989422804014327
        dz[:, at] = (nt(go[...], wr[at, :]) * slope).astype(BF16)
    dn[...] = nt(dz[...], we[...])
    acc_ref[0:chans, :] += nn(normed_t[...], dz[...])
    acc_ref[chans : 2 * chans, :] += nn(go_t[...], hid[...])

    def back(i, _):
        at = pl.ds(pl.multiple_of(i * cols, cols), cols)
        nhat = nhat_ref[at, :]
        d = dn[at, :] * gain[0:1, :]
        first = jnp.sum(d, axis=-1, keepdims=True) * (1.0 / chans)
        second = jnp.sum(d * nhat, axis=-1, keepdims=True) * (1.0 / chans)
        rstd = rstd_ref[at, :]
        g = (jnp.concatenate([rstd, rstd], axis=1) * (d - first - nhat * second)).astype(BF16)
        g_ref[step * rows + i] = g
        for h in range(2):
            gpad[h, step * rows + i + 3] = g[:, half(h)].astype(F32)
        return 0

    lax.fori_loop(0, rows, back, 0, unroll=4)

    @pl.when(step == pl.num_programs(0) - 1)
    def _():
        filter_sums(pad, gpad, taps)
        high = gpad.shape[1] - 6
        for h in range(2):
            for first, flat in ((3, g_top), (high, g_bottom)):
                for i in range(3):
                    flat[i * cols : (i + 1) * cols, half(h)] = gpad[h, first + i].astype(BF16)
            for col, flat in ((0, g_left), (cols - 3, g_right)):

                def collect(i, _, col=col, flat=flat, h=h):
                    v = [gpad[h, 3 + i * 16 + r, col : col + 3, :] for r in range(16)]
                    at = pl.ds(pl.multiple_of(i * 48, 16), 48)
                    flat[at, half(h)] = jnp.concatenate(v, axis=0).astype(BF16)
                    return 0

                lax.fori_loop(0, high // 16, collect, 0)
        blocks = hidden // LANES
        side = upper[0]
        for e in range(blocks):
            cut = half(e)
            other = acc_ref[chans : 2 * chans, cut].T
            count = 2 * TAPS // blocks
            piece = [acc_ref[0:chans, cut], other[:, :LANES], other[:, LANES:]]
            piece += [taps[e * count : (e + 1) * count, :], jnp.zeros((EXTRA - count, LANES), F32)]
            piece = jnp.concatenate(piece, axis=0)
            size = piece.shape[0]
            at = pl.ds((e % (blocks // 2)) * size, size)
            mine = side == e // (blocks // 2)

            @pl.when(mine)
            def _(piece=piece, at=at):
                kept[at, :] = piece

            @pl.when(jnp.logical_not(mine))
            def _(piece=piece, at=at):
                sent[at, :] = piece.astype(BF16)


def branch(x, halo, cot, tissue, upper, w, bias, gain, shift, we, be, wr, scale):
    rows, cols, chans = x.shape
    hidden = we.shape[1]
    pix = TILE * cols
    block = pl.BlockSpec((TILE, cols, chans), lambda s, t, u: (s, 0, 0))
    whole = lambda *shape: pl.BlockSpec(shape, lambda s, t, u: (0, 0))
    size = (2 * chans + EXTRA) * (hidden // LANES) // 2
    grid = pltpu.PrefetchScalarGridSpec(
        num_scalar_prefetch=2,
        grid=(rows // TILE,),
        in_specs=[VMEM] * 5 + [block] + [VMEM] * 8,
        out_specs=[pl.BlockSpec((rows, cols, chans), lambda s, t, u: (0, 0, 0))]
        + [whole(3 * rows, chans)] * 2
        + [whole(3 * cols, chans)] * 2
        + [whole(size, LANES)] * 2,
        scratch_shapes=[
            pltpu.VMEM((2 * TAPS, LANES), F32),
            pltpu.VMEM((2 * chans, hidden), F32),
            pltpu.VMEM((2, rows + 6, cols, LANES), F32),
            pltpu.VMEM((2, rows + 6, cols + 16, LANES), F32),
            pltpu.VMEM((2, 49, 8, LANES), F32),
            pltpu.VMEM((pix, chans), F32),
            pltpu.VMEM((pix, chans), F32),
            pltpu.VMEM((pix, LANES), F32),
            pltpu.VMEM((pix, chans), BF16),
            pltpu.VMEM((chans, pix), BF16),
            pltpu.VMEM((pix, chans), BF16),
            pltpu.VMEM((chans, pix), BF16),
            pltpu.VMEM((pix, hidden), BF16),
            pltpu.VMEM((pix, hidden), BF16),
            pltpu.VMEM((pix, chans), F32),
        ],
    )
    return pl.pallas_call(
        branch_kernel,
        grid_spec=grid,
        out_shape=(
            jax.ShapeDtypeStruct(x.shape, BF16),
            jax.ShapeDtypeStruct((3 * rows, chans), BF16),
            jax.ShapeDtypeStruct((3 * rows, chans), BF16),
            jax.ShapeDtypeStruct((3 * cols, chans), BF16),
            jax.ShapeDtypeStruct((3 * cols, chans), BF16),
            jax.ShapeDtypeStruct((size, LANES), F32),
            jax.ShapeDtypeStruct((size, LANES), BF16),
        ),
        compiler_params=pltpu.CompilerParams(vmem_limit_bytes=56 << 20),
        cost_estimate=cost(42),
        name="branch",
    )(tissue, upper, x, *halo, cot, w, bias, gain, shift, we, be, wr, scale)


def cost(us):
    return pl.CostEstimate(flops=0, transcendentals=0, bytes_accessed=int(us * 3.69e6))


def input_kernel(part, g_ref, top, bottom, left, right, cot, w_ref, *rest):
    o_ref, pad, wide, out = rest[-4:]
    rows, cols, _ = out.shape
    base = part * rows
    spread_weights(w_ref, wide, True)
    fill(pad, g_ref, top, bottom, left, right, base, rows)
    ng = cols // (8 * CB)
    for h in range(2):

        def conv(n, _):
            row, col = (n // ng) * RG, (n % ng) * (8 * CB)
            acc = stencil(pad, wide, h, row, col)
            for i in range(RG):
                for c in range(CB):
                    at = pl.ds(pl.multiple_of(col + c * 8, 8), 8)
                    out[row + i, at, half(h)] = acc[i][c]
            return 0

        lax.fori_loop(0, (rows // RG) * ng, conv, 0)

    def last(i, _):
        o_ref[i] = (cot[base + i].astype(F32) + out[i]).astype(BF16)
        return 0

    lax.fori_loop(0, rows, last, 0, unroll=4)


def input_grad(g, halo, cot, w, so_far, part):
    _, cols, chans = g.shape
    arrays = (g, *halo, cot, w)
    specs = [VMEM] * len(arrays)
    alias = {}
    if so_far is not None:
        alias = {len(arrays): 0}
        arrays += (so_far,)
        specs.append(pl.BlockSpec(memory_space=pl.ANY))
    return pl.pallas_call(
        functools.partial(input_kernel, part),
        grid=(1,),
        out_shape=jax.ShapeDtypeStruct(g.shape, BF16),
        in_specs=specs,
        out_specs=pl.BlockSpec((PART, cols, chans), lambda s: (part, 0, 0)),
        scratch_shapes=[
            pltpu.VMEM((2, PART + 6, cols + 16, LANES), F32),
            pltpu.VMEM((2, 49, 8, LANES), F32),
            pltpu.VMEM((PART, cols, chans), F32),
        ],
        input_output_aliases=alias,
        compiler_params=pltpu.CompilerParams(vmem_limit_bytes=16 << 20),
        cost_estimate=cost(4),
        name="input_grad",
    )(*arrays)


def spread_kernel(upper, mine, other, taps_ref, expand, reduce, *, factor):
    chans = expand.shape[0]
    blocks = expand.shape[1] // LANES
    size = 2 * chans + EXTRA
    count = 2 * TAPS // blocks
    for e in range(blocks):
        at = pl.ds((e % (blocks // 2)) * size, size)
        here = upper[0] == e // (blocks // 2)

        def write(flat, e=e, at=at):
            v = flat[at, :].astype(F32) * factor
            expand[:, half(e)] = v[:chans]
            for h in range(2):
                reduce[half(e), half(h)] = v[chans + h * LANES : chans + (h + 1) * LANES]
            h, first = e * count // TAPS, e * count % TAPS
            lines = min(count, taps_ref.shape[0] - first)
            taps_ref[first : first + lines, half(h)] = v[2 * chans : 2 * chans + lines]

        pl.when(here)(functools.partial(write, mine))
        pl.when(jnp.logical_not(here))(functools.partial(write, other))


def spread(upper, mine, other, taps, chans, hidden, factor):
    grid = pltpu.PrefetchScalarGridSpec(
        num_scalar_prefetch=1,
        grid=(1,),
        in_specs=[VMEM] * 2,
        out_specs=[
            pl.BlockSpec(shape, lambda s, u: (0, 0))
            for shape in ((taps, chans), (chans, hidden), (hidden, chans))
        ],
    )
    return pl.pallas_call(
        functools.partial(spread_kernel, factor=factor),
        grid_spec=grid,
        out_shape=(
            jax.ShapeDtypeStruct((taps, chans), F32),
            jax.ShapeDtypeStruct((chans, hidden), F32),
            jax.ShapeDtypeStruct((hidden, chans), F32),
        ),
        compiler_params=pltpu.CompilerParams(vmem_limit_bytes=12 << 20),
        cost_estimate=cost(2),
        name="spread",
    )(upper, mine, other)


AXES = ("y", "x_hi", "core", "z", "x_lo")
SIZES = (4, 2, 2, 8, 2)
TY, TX = AXES[:3], AXES[3:]


def beside(value, axes, odd):
    count = math.prod(SIZES[AXES.index(a)] for a in axes)
    pairs = [(i, i + 1) for i in range(odd, count - 1, 2)]
    return lax.ppermute(value, axes, pairs + [(b, a) for a, b in pairs])


def both_sides(low, high, axes):
    odd = lax.axis_index(axes) % 2 == 1
    first = beside(jnp.where(odd, low, high), axes, 0)
    second = beside(jnp.where(odd, high, low), axes, 1)
    return jnp.where(odd, first, second), jnp.where(odd, second, first)


def halo_of(left, right, top, bottom):
    chans = left.shape[1]
    left, right = both_sides(left, right, TX)
    filler = jnp.zeros((14, chans), BF16)
    top = jnp.concatenate([top, left[:9], right[:9], filler])
    bottom = jnp.concatenate([bottom, left[-9:], right[-9:], filler])
    top, bottom = both_sides(top, bottom, TY)
    return top, bottom, left, right


SWAPS = {
    "core": (("core",), ("core",)),
    "x_near": (("x_lo",), ("x_lo", "x_hi")),
    "x_far": (("x_lo", "x_hi"), ("x_hi",)),
    "y_near": ((("y", 1),), (("y", 1), ("y", 2))),
    "y_far": ((("y", 3),), (("y", 2),)),
}


def keeps_upper(name):
    bit = 0
    for item in SWAPS[name][1]:
        axis, mask = item if isinstance(item, tuple) else (item, 1)
        bit = bit + (lax.axis_index(axis) // mask) % 2
    return bit % 2


def swap(value, name):
    index = np.arange(math.prod(SIZES)).reshape(SIZES)
    where = np.indices(SIZES)
    for item in SWAPS[name][0]:
        axis, mask = item if isinstance(item, tuple) else (item, 1)
        where[AXES.index(axis)] ^= mask
    other = index[tuple(where)]
    pairs = [(int(a), int(b)) for a, b in zip(index.ravel(), other.ravel())]
    return lax.ppermute(value, AXES, pairs)


def total(kept, sent):
    names = list(SWAPS)
    for n, name in enumerate(names):
        kept = kept + swap(sent, name).astype(F32)
        if n + 1 < len(names):
            upper = keeps_upper(names[n + 1]) == 1
            size = kept.shape[0] // 2
            low, high = kept[:size], kept[size:]
            sent = jnp.where(upper, low, high).astype(BF16)
            kept = jnp.where(upper, high, low)
    count = SIZES[AXES.index("z")]
    copies = jnp.broadcast_to(kept.astype(BF16)[None], (count, *kept.shape))
    copies = lax.all_to_all(copies, "z", 0, 0, tiled=True)
    out = jnp.sum(copies.astype(F32), axis=0).astype(BF16)
    for name in reversed(names):
        upper = keeps_upper(name) == 1
        other = swap(out, name)
        if name == "core":
            return out, other
        out = jnp.concatenate([jnp.where(upper, other, out), jnp.where(upper, out, other)])


def body(x, cot, tissue, w, bias, gain, shift, we, be, wr, scale):
    rows, cols, chans = x.shape
    line = lambda v: v.reshape(1, -1)
    sizes = (math.prod(SIZES[:3]), math.prod(SIZES[3:]))
    factor = 1.0 / math.sqrt(rows * sizes[0] * cols * sizes[1])
    edges = (x[:, :3], x[:, cols - 3 :], x[:3], x[rows - 3 :])
    halo = halo_of(*(v.reshape(-1, chans) for v in edges))
    upper = keeps_upper("core").astype(jnp.int32).reshape(1)
    rest = (w, line(bias), line(gain), line(shift), we, line(be), wr, line(scale))
    g, *edges, kept, sent = branch(x, halo, cot, tissue, upper, *rest)
    ghalo = halo_of(*edges)
    result = None
    for part in range(rows // PART):
        result = input_grad(g, ghalo, cot, w, result, part)
    mine, other = total(kept, sent)
    sums = spread(upper, mine, other, w.shape[0], chans, we.shape[1], factor)
    return (result, *sums)


def solution(mesh):
    fine = Mesh(mesh.devices.reshape(SIZES), AXES)
    pixels = P(TY, TX, None)
    return jax.shard_map(
        body,
        mesh=fine,
        in_specs=(pixels, pixels, P(TY, TX)) + (P(),) * 8,
        out_specs=(pixels, P(), P(), P()),
        check_vma=False,
    )
```
